128 devices in a mesh: dp: 16 (over y, z), seq: 8 (over x, core).
Axes of the slice: x: 4, y: 4, z: 4, core: 2. Of those that a mesh axis runs over, the one named last changes fastest.
Arguments:
- queries: bfloat16 [16, 1024, 4096], P('dp', 'seq'), may hold values from -12 to 12
- key_states: bfloat16 [16, 1024, 512], P('dp', 'seq'), may hold values from -12 to 12
- value_states: bfloat16 [16, 1024, 512], P('dp', 'seq'), may hold values from -6 to 6
- out_grad: bfloat16 [16, 1024, 4096], P('dp', 'seq'), may hold values from -6 to 6
- layer_input: bfloat16 [16, 1024, 8192], P('dp', 'seq'), may hold values from -6 to 6
- lengths: int32 [16, 8], P('dp'), may hold values from 1 to 512, 1024 in all within a row
Outputs:
- query_grad: bfloat16 [16, 1024, 4096], P('dp', 'seq')
- key_grad: bfloat16 [16, 1024, 512], P('dp', 'seq')
- value_grad: bfloat16 [16, 1024, 512], P('dp', 'seq')
- value_weight_grad: float32 [8192, 512], P(('dp', 'seq'))
The draws below stay inside these ranges and needn't reach their ends.
Inputs may be any that keep to these rules, and one draw needn't show every extreme that they name: `lengths`: each row sums to 1024 and its largest entry is exactly 512.
All inputs are finite; a program needn't handle non-finite values.
Results may differ from the reference program's by a relative error of at most 0.018.
Values may be sent and summed in bfloat16 or wider, within the bound.
No kernel may reach another device: no remote copies, remote signals or barrier semaphores. Data moves between devices by JAX's collectives and lax.ppermute only.
A program may use at most 192 MiB of HBM per device.

```python
import math
import jax
import jax.numpy as jnp
import numpy as np
from jax import lax

D = 8192
HQ = 32
HK = 4
HD = 128
LEN = 1024
SAMPLES = 8
STREAMS = 16
MOST = 512


def draw_queries(key, part):
    gaussian = jax.random.normal(jax.random.fold_in(key, 11), (STREAMS, LEN, HQ, HD), jnp.float32)
    return jnp.clip(gaussian, -12.0, 12.0).reshape(STREAMS, LEN, HQ * HD).astype(jnp.bfloat16)


def draw_key_states(key, part):
    gaussian = jax.random.normal(jax.random.fold_in(key, 13), (STREAMS, LEN, HK, HD), jnp.float32)
    return jnp.clip(gaussian, -12.0, 12.0).reshape(STREAMS, LEN, HK * HD).astype(jnp.bfloat16)


def shard_levels(own_key, dims, cuts, smallest, largest):
    factor_of, own = 1.0, jax.random.fold_in(own_key, 6)
    for axis_at, blocks in cuts:
        steps = jnp.exp(jax.random.uniform(jax.random.fold_in(own, axis_at), (blocks,), jnp.float32, smallest / len(cuts), largest / len(cuts)))
        factor_of = factor_of * jnp.repeat(steps, dims[axis_at] // blocks).reshape([-1 if axis == axis_at else 1 for axis in range(len(dims))])
    return factor_of


def profile(number_of, total, most, slope):
    loads = [(1 << 20) // math.isqrt(standing ** slope) + 1 for standing in range(2, number_of + 1)]
    spare, given = total - most - (number_of - 1), [1] * (number_of - 1)
    while spare > 0:
        candidates = [i for i in range(number_of - 1) if given[i] < most]
        mass, budget = sum([loads[i] for i in candidates]), spare
        for i in candidates:
            addition = min(most - given[i], max(1, budget * loads[i] // mass), spare)
            given[i] = given[i] + addition
            spare = spare - addition
    return np.array([most] + given)


def ragged(own_key, count, total, limit, lean):
    if count == 2:
        one = jax.random.randint(own_key, (), max(1, total - limit), min(limit, total - 1) + 1)
        return jnp.stack([one, total - one])
    sizes = jnp.asarray(profile(count, total, limit, lean), jnp.int32)
    pairs = (count - 1) // 2
    donor, sink = sizes[1:1 + 2 * pairs:2], sizes[2:2 + 2 * pairs:2]
    slack = jnp.minimum(donor - 1, limit - sink)
    moved = jax.random.randint(jax.random.fold_in(own_key, 1), (pairs,), 0, 1 << 20) % (slack + 1)
    sizes = sizes.at[1:1 + 2 * pairs:2].set(donor - moved).at[2:2 + 2 * pairs:2].set(sink + moved)
    return sizes[jax.random.permutation(jax.random.fold_in(own_key, 2), count)]


def normal_values(stream_key, dims, width, limit, cuts=(), kind=jnp.bfloat16):
    values = jax.random.normal(stream_key, dims, jnp.float32) * width
    if len(cuts) > 0:
        values = shard_levels(stream_key, dims, cuts, -0.22, 0.18) * values
    return jnp.clip(values, min=-limit, max=limit).astype(kind)


def setup_inputs(seed: int = 0) -> dict:
    splits = jax.random.split(jax.random.key(seed), 7)
    queries = draw_queries(jax.random.fold_in(splits[6], 71), 0)
    key_states = draw_key_states(jax.random.fold_in(splits[6], 71), 0)
    value_states = normal_values(splits[2], (STREAMS, LEN, HK * HD), 1.0, 6.0, ((0, 16), (1, 8)))
    out_grad = normal_values(splits[3], (STREAMS, LEN, HQ * HD), 1.0, 6.0, ((0, 16), (1, 8)))
    layer_input = normal_values(splits[4], (STREAMS, LEN, D), 1.0, 6.0, ((0, 16), (1, 8)))
    lengths = jax.vmap(lambda own: ragged(own, SAMPLES, LEN, MOST, 2))(jax.random.split(splits[5], STREAMS)).reshape((STREAMS, SAMPLES)).astype(jnp.int32)
    return {"queries": queries, "key_states": key_states, "value_states": value_states, "out_grad": out_grad, "layer_input": layer_input, "lengths": lengths}


def segment_ids_of(lengths):
    sample_ends = jnp.cumsum(lengths).astype(jnp.int32)
    positions = jnp.arange(LEN, dtype=jnp.int32)
    return lax.optimization_barrier(jnp.sum((sample_ends[None, :] <= positions[:, None]).astype(jnp.int32), axis=1))

def stream_grads(operands):
    queries, key_states, value_states, out_grad, lengths = operands
    group_size = HQ // HK
    score_scale = HD ** (-0.5)
    segment_ids = segment_ids_of(lengths)
    positions = jnp.arange(LEN, dtype=jnp.int32)
    allowed = (segment_ids[:, None] == segment_ids[None, :]) & (positions[None, :] <= positions[:, None])
    query_all = queries.reshape(LEN, HK, group_size, HD)
    grad_all = out_grad.reshape(LEN, HK, group_size, HD)
    key_all = key_states.reshape(LEN, HK, HD)
    value_all = value_states.reshape(LEN, HK, HD)
    query_list, key_list, value_list = ([], [], [])
    for group_index in range(HK):
        query_group = query_all[:, group_index].astype(jnp.float32)
        grad_group = grad_all[:, group_index].astype(jnp.float32)
        key_group = key_all[:, group_index].astype(jnp.float32)
        value_group = value_all[:, group_index].astype(jnp.float32)
        scores = jnp.einsum('qgd,kd->gqk', query_group, key_group) * score_scale
        scores = jnp.where(allowed[None], scores, -jnp.inf)
        row_peak = lax.optimization_barrier(jnp.max(scores, axis=-1, keepdims=True))
        exponent = jnp.exp(scores - row_peak)
        attn_weights = exponent / lax.optimization_barrier(jnp.sum(exponent, axis=-1, keepdims=True))
        prob_grad = jnp.einsum('qgd,kd->gqk', grad_group, value_group)
        row_delta = lax.optimization_barrier(jnp.sum(attn_weights * prob_grad, axis=-1, keepdims=True))
        score_grad = (attn_weights * (prob_grad - row_delta) * score_scale).astype(jnp.bfloat16)
        weights_half = attn_weights.astype(jnp.bfloat16)
        query_list.append(jnp.einsum('gqk,kd->qgd', score_grad.astype(jnp.float32), key_group).astype(jnp.bfloat16))
        key_part = jnp.einsum('gqk,qgd->gkd', score_grad.astype(jnp.float32), query_group).astype(jnp.bfloat16)
        value_part = jnp.einsum('gqk,qgd->gkd', weights_half.astype(jnp.float32), grad_group).astype(jnp.bfloat16)
        key_list.append(lax.optimization_barrier(jnp.sum(key_part.astype(jnp.float32), axis=0)).astype(jnp.bfloat16))
        value_list.append(lax.optimization_barrier(jnp.sum(value_part.astype(jnp.float32), axis=0)).astype(jnp.bfloat16))
    query_grad = jnp.stack(query_list, axis=1).reshape(LEN, HQ * HD)
    key_grad = jnp.stack(key_list, axis=1).reshape(LEN, HK * HD)
    value_grad = jnp.stack(value_list, axis=1).reshape(LEN, HK * HD)
    return (query_grad, key_grad, value_grad)

def reference(queries, key_states, value_states, out_grad, layer_input, lengths):
    query_grad, key_grad, value_grad = lax.map(stream_grads, (queries, key_states, value_states, out_grad, lengths))
    flat_input = layer_input.reshape(STREAMS * LEN, D)
    flat_value = value_grad.reshape(STREAMS * LEN, HK * HD)
    weight_sum = jnp.dot(flat_input.T, flat_value, preferred_element_type=jnp.float32)
    value_weight_grad = weight_sum / math.sqrt(STREAMS * LEN)
    return (query_grad, key_grad, value_grad, value_weight_grad)
```

```python
import math

import jax
import jax.numpy as jnp
from jax import lax
from jax.experimental import pallas as pl
from jax.experimental.pallas import tpu as pltpu
from jax.sharding import Mesh, PartitionSpec as P

D = 8192
HQ = 32
HK = 4
HD = 128
LEN = 1024
BLK = 128
NBLK = LEN // BLK
WIN = 5
SCALE = HD ** (-0.5)
EXP2_SCALE = SCALE * math.log2(math.e)
MASKED = -1e30
GROUP = HQ // HK
NT = (((1,), (1,)), ((), ()))
NN = (((1,), (0,)), ((), ()))


def dot(a, b, dims):
    return lax.dot_general(a, b, dims, preferred_element_type=jnp.float32)


def attention_kernel(
    info, q_own, do_own, q_oth, do_oth, k_ref, v_ref,
    dq_own, dq_oth, dk_ref, dv_ref,
    k_t, dk_acc, dv_acc, bias_ref,
):
    chip, core = info[0], info[1]
    k_t[...] = k_ref[...].reshape(LEN, HD).T
    dk_acc[...] = jnp.zeros_like(dk_acc)
    dv_acc[...] = jnp.zeros_like(dv_acc)
    for tile in range(2):
        q_ref, do_ref, dq_ref = ((q_own, do_own, dq_own), (q_oth, do_oth, dq_oth))[tile]
        block = 2 * chip + (core if tile == 0 else 1 - core)
        first = jnp.maximum(block - (WIN - 1), 0)
        rows = pl.ds(pl.multiple_of(first * BLK, BLK), WIN * BLK)
        k_pos = first * BLK + lax.broadcasted_iota(jnp.int32, (WIN * BLK, 2 * BLK), 0)
        lane = lax.broadcasted_iota(jnp.int32, (1, 2 * BLK), 1)
        q_pos = block * BLK + (lane & (BLK - 1))
        begin = jnp.zeros_like(q_pos)
        end = jnp.int32(0)
        for sample in range(8):
            end = end + info[2 + sample]
            begin = jnp.where(end <= q_pos, end, begin)
        allowed = (k_pos >= begin) & (k_pos <= q_pos)
        bias_ref[...] = jnp.where(allowed, 0.0, MASKED)
        k_win = k_ref[pl.ds(first, WIN)].reshape(WIN * BLK, HD)
        v_win = v_ref[pl.ds(first, WIN)].reshape(WIN * BLK, HD)
        for pair in range(GROUP // 2):
            cols = [slice((2 * pair + i) * HD, (2 * pair + i + 1) * HD) for i in range(2)]
            q_two = jnp.concatenate([q_ref[:, c] for c in cols], axis=0)
            do_two = jnp.concatenate([do_ref[:, c] for c in cols], axis=0)
            scores = dot(k_win, q_two, NT) * EXP2_SCALE + bias_ref[...]
            exponent = jnp.exp2(scores - jnp.max(scores, axis=0, keepdims=True))
            probs = exponent * (1.0 / jnp.sum(exponent, axis=0, keepdims=True))
            dprobs = dot(v_win, do_two, NT)
            delta = jnp.sum(probs * dprobs, axis=0, keepdims=True)
            dscores = (probs * (dprobs - delta)).astype(jnp.bfloat16)
            dv_acc[rows, :] += dot(probs.astype(jnp.bfloat16), do_two, NN)
            dk_acc[rows, :] += dot(dscores, q_two, NN)
            dq_t = dot(k_t[:, rows], dscores, NN) * SCALE
            for i in range(2):
                dq_ref[:, cols[i]] = dq_t[:, i * BLK : (i + 1) * BLK].T.astype(jnp.bfloat16)
    dk_ref[...] = (dk_acc[...] * SCALE).astype(jnp.bfloat16).reshape(dk_ref.shape)
    dv_ref[...] = dv_acc[...].astype(jnp.bfloat16).reshape(dv_ref.shape)


def attention(info, queries, out_grad, others, kv):
    width = GROUP * HD
    half = HQ * HD // 2
    own = pl.BlockSpec((BLK, width), lambda g, s: (0, s[1] * 2 + g))

    def other(which):
        return pl.BlockSpec((None, BLK, width), lambda g, s: (which, 0, g))

    def keys(which):
        return pl.BlockSpec((NBLK, None, BLK, HD), lambda g, s: (0, which, 0, g))

    part = pl.BlockSpec((NBLK, BLK, HD), lambda g, s: (0, 0, g))
    part_shape = jax.ShapeDtypeStruct((NBLK, BLK, 2 * HD), jnp.bfloat16)
    return pl.pallas_call(
        attention_kernel,
        grid_spec=pltpu.PrefetchScalarGridSpec(
            num_scalar_prefetch=1,
            grid=(2,),
            in_specs=[own, own, other(0), other(1), keys(0), keys(1)],
            out_specs=[own, pl.BlockSpec((BLK, width), lambda g, s: (0, g)), part, part],
            scratch_shapes=[
                pltpu.VMEM((HD, LEN), jnp.bfloat16),
                pltpu.VMEM((LEN, HD), jnp.float32),
                pltpu.VMEM((LEN, HD), jnp.float32),
                pltpu.VMEM((WIN * BLK, 2 * BLK), jnp.float32),
            ],
        ),
        out_shape=[
            jax.ShapeDtypeStruct((BLK, HQ * HD), jnp.bfloat16),
            jax.ShapeDtypeStruct((BLK, half), jnp.bfloat16),
            part_shape,
            part_shape,
        ],
        name="attention_backward",
    )(info, queries, out_grad, others, others, kv, kv)


SWAP = [(0, 1), (1, 0)]


def shards(queries, key_states, value_states, out_grad, layer_input, lengths):
    chip, core = lax.axis_index("x"), lax.axis_index("core")
    queries, out_grad = queries[0], out_grad[0]
    half = HQ * HD // 2

    kv = jnp.stack([key_states[0], value_states[0]]).reshape(2, BLK, 2, 2 * HD)
    kv = jnp.broadcast_to(jnp.moveaxis(kv, 2, 0)[None], (4, 2, 2, BLK, 2 * HD))
    kv = lax.all_to_all(kv.reshape(NBLK, 2, BLK, 2 * HD), ("x", "core"), 0, 0, tiled=True)

    def other_half(a):
        return lax.dynamic_slice(a, (0, (1 - core) * half), (BLK, half))

    others = lax.ppermute(jnp.stack([other_half(queries), other_half(out_grad)]), "core", SWAP)

    x_z = lax.all_to_all(layer_input[0].reshape(BLK, 4, 4, D // 16), "z", 2, 0, tiled=True)
    x_own = x_z.reshape(4 * BLK, D // 4)
    x_oth = lax.ppermute(x_own, "core", SWAP)

    info = jnp.concatenate([jnp.stack([chip, core]).astype(jnp.int32), lengths[0]])
    dq_own, dq_oth, dk, dv = attention(info, queries, out_grad, others, kv)

    dv = lax.all_to_all(dv.reshape(4, 2 * BLK, 2 * HD), "x", 0, 0, tiled=True)
    dv = jnp.sum(dv.astype(jnp.float32), axis=0).astype(jnp.bfloat16)

    dv_z = lax.all_to_all(jnp.broadcast_to(dv[None], (4, 2 * BLK, 2 * HD)), "z", 0, 0, tiled=True)
    dv_z = dv_z.reshape(4, 2, BLK, 2 * HD)
    dv_own = lax.dynamic_index_in_dim(dv_z, core, 1, False).reshape(4 * BLK, 2 * HD)
    dv_oth = lax.dynamic_index_in_dim(dv_z, 1 - core, 1, False).reshape(4 * BLK, 2 * HD)
    over_tokens = (((0,), (0,)), ((), ()))
    weight = dot(x_own, dv_own, over_tokens) + dot(x_oth, dv_oth, over_tokens)
    weight = weight.astype(jnp.bfloat16).reshape(32, 64, 2 * HD)
    weight = lax.all_to_all(weight, ("y", "x", "core"), 0, 0, tiled=True)
    weight = jnp.sum(weight.reshape(16, 2, 64, 2 * HD).astype(jnp.float32), axis=0)
    weight = jnp.moveaxis(weight, 0, 1).reshape(64, HK * HD) / math.sqrt(16 * LEN)

    dq_got = lax.ppermute(dq_oth, "core", SWAP)
    query_grad = lax.dynamic_update_slice(dq_own, dq_got, (0, (1 - core) * half))

    dk = lax.all_to_all(dk, ("x", "core"), 0, 0, tiled=True)
    dk = jnp.sum(dk.reshape(4, 2, BLK, 2 * HD).astype(jnp.float32), axis=0)
    key_grad = jnp.moveaxis(dk.astype(jnp.bfloat16), 0, 1).reshape(BLK, HK * HD)

    dv_rows = dv.reshape(2, BLK, 2 * HD)
    dv_keep = lax.dynamic_index_in_dim(dv_rows, core, 0, False)
    dv_got = lax.ppermute(lax.dynamic_index_in_dim(dv_rows, 1 - core, 0, False), "core", SWAP)
    low = jnp.where(core == 0, dv_keep, dv_got)
    high = jnp.where(core == 0, dv_got, dv_keep)
    value_grad = jnp.concatenate([low, high], axis=1)
    return query_grad[None], key_grad[None], value_grad[None], weight


def solution(mesh):
    whole = Mesh(mesh.devices.reshape(4, 4, 4, 2), ("y", "z", "x", "core"))
    rows = P(("y", "z"), ("x", "core"), None)
    return jax.shard_map(
        shards,
        mesh=whole,
        in_specs=(rows,) * 5 + (P(("y", "z"), None),),
        out_specs=(rows,) * 3 + (P(("y", "z", "x", "core"), None),),
        check_vma=False,
    )
```

```python
import math

import jax
import jax.numpy as jnp
from jax import lax
from jax.experimental import pallas as pl
from jax.experimental.pallas import tpu as pltpu
from jax.sharding import Mesh, PartitionSpec as P


D = 8192
HQ = 32
HK = 4
HD = 128
LEN = 1024
BLK = 128
SPAN = 6
WIN = 5
GROUP = HQ // HK
HALF = HQ * HD // 2
COLS = 2 * HD
FEAT = D // 16
SCALE = HD ** (-0.5)
EXP2_SCALE = SCALE * math.log2(math.e)
MASKED = -1e30
NT = (((1,), (1,)), ((), ()))
NN = (((1,), (0,)), ((), ()))
TN = (((0,), (0,)), ((), ()))
SWAP = [(0, 1), (1, 0)]
BF16 = jnp.bfloat16


def dot(a, b, dims):
    return lax.dot_general(a, b, dims, preferred_element_type=jnp.float32)


def pack_kernel(x_ref, out_ref, buf, sem_in, sem_out):
    pieces = [(z, y) for z in range(4) for y in range(4)]
    loads, stores = [], []
    for i, (z, y) in enumerate(pieces):
        cols = pl.ds((y * 4 + z) * FEAT, FEAT)
        loads.append(pltpu.make_async_copy(x_ref.at[:, cols], buf.at[i], sem_in.at[i]))
        stores.append(pltpu.make_async_copy(buf.at[i], out_ref.at[z, y], sem_out.at[i]))
        loads[-1].start()
    for load, store in zip(loads, stores):
        load.wait()
        store.start()
    for store in stores:
        store.wait()


def pack(layer_input):
    return pl.pallas_call(
        pack_kernel,
        in_specs=[pl.BlockSpec(memory_space=pl.ANY)],
        out_specs=pl.BlockSpec(memory_space=pl.ANY),
        out_shape=jax.ShapeDtypeStruct((4, 4, BLK, FEAT), BF16),
        scratch_shapes=[
            pltpu.VMEM((16, BLK, FEAT), BF16),
            pltpu.SemaphoreType.DMA((16,)),
            pltpu.SemaphoreType.DMA((16,)),
        ],
        cost_estimate=pl.CostEstimate(flops=0, transcendentals=0, bytes_accessed=4 << 20),
        name="pack",
    )(layer_input)


def attention_kernel(
    info, q_own, do_own, q_oth, do_oth, kv_two, kv_one, kv_here,
    dq_own, dq_oth, dk_two, dk_one, dk_here, dv_two, dv_one, dv_here,
    k_buf, v_buf, k_t, dk_acc, dv_acc, bias_ref,
):
    chip, core = info[0], info[1]
    for j, kv in enumerate((kv_two, kv_one, kv_here)):
        for side in range(2):
            place = 2 * j + (core if side == 0 else 1 - core)
            k_buf[place] = kv[side, 0]
            v_buf[place] = kv[side, 1]
    k_t[...] = k_buf[...].reshape(SPAN * BLK, HD).T
    dk_acc[...] = jnp.zeros_like(dk_acc)
    dv_acc[...] = jnp.zeros_like(dv_acc)
    for side in range(2):
        q_ref, do_ref, dq_ref = ((q_own, do_own, dq_own), (q_oth, do_oth, dq_oth))[side]
        parity = core if side == 0 else 1 - core
        rows = pl.ds(pl.multiple_of(parity * BLK, BLK), WIN * BLK)
        k_pos = (2 * chip - 4 + parity) * BLK + lax.broadcasted_iota(
            jnp.int32, (WIN * BLK, 2 * BLK), 0
        )
        lane = lax.broadcasted_iota(jnp.int32, (1, 2 * BLK), 1)
        q_pos = (2 * chip + parity) * BLK + (lane & (BLK - 1))
        begin = jnp.zeros_like(q_pos)
        end = jnp.int32(0)
        for sample in range(8):
            end = end + info[2 + sample]
            begin = jnp.where(end <= q_pos, end, begin)
        allowed = (k_pos >= begin) & (k_pos <= q_pos)
        bias_ref[...] = jnp.where(allowed, 0.0, MASKED)
        k_win = k_buf[pl.ds(parity, WIN)].reshape(WIN * BLK, HD)
        v_win = v_buf[pl.ds(parity, WIN)].reshape(WIN * BLK, HD)
        for pair in range(GROUP // 2):
            cols = [slice((2 * pair + i) * HD, (2 * pair + i + 1) * HD) for i in range(2)]
            q_two = jnp.concatenate([q_ref[:, c] for c in cols], axis=0)
            do_two = jnp.concatenate([do_ref[:, c] for c in cols], axis=0)
            scores = dot(k_win, q_two, NT) * EXP2_SCALE + bias_ref[...]
            exponent = jnp.exp2(scores - jnp.max(scores, axis=0, keepdims=True))
            probs = exponent * (1.0 / jnp.sum(exponent, axis=0, keepdims=True))
            dprobs = dot(v_win, do_two, NT)
            delta = jnp.sum(probs * dprobs, axis=0, keepdims=True)
            dscores = (probs * (dprobs - delta)).astype(BF16)
            dv_acc[rows, :] += dot(probs.astype(BF16), do_two, NN)
            dk_acc[rows, :] += dot(dscores, q_two, NN)
            dq_t = dot(k_t[:, rows], dscores, NN) * SCALE
            for i in range(2):
                dq_ref[:, cols[i]] = dq_t[:, i * BLK : (i + 1) * BLK].T.astype(BF16)
    for j, (dk, dv) in enumerate(((dk_two, dv_two), (dk_one, dv_one), (dk_here, dv_here))):
        for side in range(2):
            place = 2 * j + (core if side == 0 else 1 - core)
            rows = pl.ds(pl.multiple_of(place * BLK, BLK), BLK)
            dk[side] = (dk_acc[rows, :] * SCALE).astype(dk.dtype)
            dv[side] = dv_acc[rows, :].astype(dv.dtype)


def attention(info, queries, out_grad, others, kv_two, kv_one, kv_here):
    width = GROUP * HD
    own = pl.BlockSpec((BLK, width), lambda g, s: (0, s[1] * 2 + g))
    sent = pl.BlockSpec((BLK, width), lambda g, s: (0, g))
    kv = pl.BlockSpec((2, 2, BLK, HD), lambda g, s: (0, 0, 0, g))
    part = pl.BlockSpec((2, BLK, HD), lambda g, s: (0, 0, g))

    def other(which):
        return pl.BlockSpec((None, BLK, width), lambda g, s: (which, 0, g))

    def part_shape(kind):
        return jax.ShapeDtypeStruct((2, BLK, COLS), kind)

    parts = [part_shape(BF16), part_shape(BF16), part_shape(jnp.float32)]
    return pl.pallas_call(
        attention_kernel,
        grid_spec=pltpu.PrefetchScalarGridSpec(
            num_scalar_prefetch=1,
            grid=(2,),
            in_specs=[own, own, other(0), other(1), kv, kv, kv],
            out_specs=[own, sent] + [part] * 6,
            scratch_shapes=[
                pltpu.VMEM((SPAN, BLK, HD), BF16),
                pltpu.VMEM((SPAN, BLK, HD), BF16),
                pltpu.VMEM((HD, SPAN * BLK), BF16),
                pltpu.VMEM((SPAN * BLK, HD), jnp.float32),
                pltpu.VMEM((SPAN * BLK, HD), jnp.float32),
                pltpu.VMEM((WIN * BLK, 2 * BLK), jnp.float32),
            ],
        ),
        out_shape=[
            jax.ShapeDtypeStruct((BLK, HQ * HD), BF16),
            jax.ShapeDtypeStruct((BLK, HALF), BF16),
        ]
        + parts
        + parts,
        cost_estimate=pl.CostEstimate(
            flops=10 * 16 * 2 * BLK * WIN * BLK * HD,
            transcendentals=16 * 2 * BLK * WIN * BLK,
            bytes_accessed=6 << 20,
        ),
        name="attention_backward",
    )(info, queries, out_grad, others, others, kv_two, kv_one, kv_here)


def weight_kernel(info, x_own, x_oth, *refs):
    dv, out_ref = refs[:-1], refs[-1]
    z = info[0]
    x_rows, dv_rows = [], []
    for back in range(4):
        source = lax.rem(z + 4 - back, 4)
        for side, x in enumerate((x_own, x_oth)):
            x_rows.append(x[source])
            dv_rows.append(dv[back][side])
    total = dot(jnp.concatenate(x_rows, axis=0), jnp.concatenate(dv_rows, axis=0), TN)
    out_ref[...] = total.astype(BF16)


def weight_part(z, x_own, x_oth, dv):
    x_spec = pl.BlockSpec((4, None, BLK, FEAT), lambda y, s: (0, y, 0, 0))
    dv_spec = pl.BlockSpec((2, BLK, COLS), lambda y, s: (0, 0, 0))
    return pl.pallas_call(
        weight_kernel,
        grid_spec=pltpu.PrefetchScalarGridSpec(
            num_scalar_prefetch=1,
            grid=(4,),
            in_specs=[x_spec, x_spec] + [dv_spec] * 4,
            out_specs=pl.BlockSpec((FEAT, COLS), lambda y, s: (y, 0)),
        ),
        out_shape=jax.ShapeDtypeStruct((4 * FEAT, COLS), BF16),
        cost_estimate=pl.CostEstimate(
            flops=2 * 4 * FEAT * COLS * 8 * BLK, transcendentals=0, bytes_accessed=6 << 20
        ),
        name="weight_part",
    )(jnp.reshape(z, (1,)).astype(jnp.int32), x_own, x_oth, *dv)


def hop(value, axis, moves):
    return lax.ppermute(value, axis, moves)


def exchange(value, axes):
    return lax.all_to_all(value, axes, 0, 0, tiled=True)


def shards(queries, key_states, value_states, out_grad, layer_input, lengths):
    chip, core, depth = lax.axis_index("x"), lax.axis_index("core"), lax.axis_index("z")
    queries, out_grad = queries[0], out_grad[0]

    def half(a, which, width):
        return lax.dynamic_slice(a, (0, which * width), (BLK, width))

    def pairs(a, b, which, width):
        return jnp.stack([half(a, which, width), half(b, which, width)])

    kv_keep = pairs(key_states[0], value_states[0], core, COLS)
    kv_send = pairs(key_states[0], value_states[0], 1 - core, COLS)
    kv_here = jnp.stack([kv_keep, hop(kv_send, "core", SWAP)])
    kv_one = hop(kv_here, "x", [(0, 1), (1, 2), (2, 3)])
    kv_two = hop(kv_here, "x", [(0, 2), (1, 3)])

    others = hop(pairs(queries, out_grad, 1 - core, HALF), "core", SWAP)

    x_own = exchange(pack(layer_input[0]), "z")
    x_oth = hop(x_own, "core", SWAP)

    info = jnp.concatenate([jnp.stack([chip, core]).astype(jnp.int32), lengths[0]])
    dq_own, dq_oth, dk_two, dk_one, dk_here, dv_two, dv_one, dv_here = attention(
        info, queries, out_grad, others, kv_two, kv_one, kv_here
    )

    def summed(here, one, two):
        one = hop(one, "x", [(1, 0), (2, 1), (3, 2)])
        two = hop(two, "x", [(2, 0), (3, 1)])
        return (here + one.astype(jnp.float32) + two.astype(jnp.float32)).astype(BF16)

    dv = summed(dv_here, dv_one, dv_two)
    dv_z = [dv] + [hop(dv, "z", [(i, (i + away) % 4) for i in range(4)]) for away in (1, 2, 3)]
    weight = weight_part(depth, x_own, x_oth, dv_z)
    weight = exchange(weight.reshape(32, 64, COLS), ("y", "x", "core"))
    weight = jnp.sum(weight.reshape(16, 2, 64, COLS).astype(jnp.float32), axis=0)
    weight = jnp.moveaxis(weight, 0, 1).reshape(64, HK * HD) / math.sqrt(16 * LEN)

    dk = summed(dk_here, dk_one, dk_two)

    dq_got = hop(dq_oth, "core", SWAP)
    query_grad = lax.dynamic_update_slice(dq_own, dq_got, (0, (1 - core) * HALF))
    got = hop(jnp.stack([dk[1], dv[1]]), "core", SWAP)

    def in_order(keep, other):
        first = jnp.where(core == 0, keep, other)
        second = jnp.where(core == 0, other, keep)
        return jnp.concatenate([first, second], axis=1)

    key_grad, value_grad = in_order(dk[0], got[0]), in_order(dv[0], got[1])
    return query_grad[None], key_grad[None], value_grad[None], weight


def solution(mesh):
    whole = Mesh(mesh.devices.reshape(4, 4, 4, 2), ("y", "z", "x", "core"))
    rows = P(("y", "z"), ("x", "core"), None)
    return jax.shard_map(
        shards,
        mesh=whole,
        in_specs=(rows,) * 5 + (P(("y", "z"), None),),
        out_specs=(rows,) * 3 + (P(("y", "z", "x", "core"), None),),
        check_vma=False,
    )
```

```python
import math

import jax
import jax.numpy as jnp
from jax import lax
from jax.experimental import pallas as pl
from jax.experimental.pallas import tpu as pltpu
from jax.sharding import Mesh, PartitionSpec as P


D = 8192
HQ = 32
HK = 4
HD = 128
LEN = 1024
BLK = 128
SPAN = 6
WIN = 5
GROUP = HQ // HK
PAIRS = GROUP // 2
WIDTH = GROUP * HD
HALF = HQ * HD // 2
COLS = 2 * HD
FEAT = D // 16
SCALE = HD ** (-0.5)
EXP2_SCALE = SCALE * math.log2(math.e)
MASKED = -1e30
NT = (((1,), (1,)), ((), ()))
NN = (((1,), (0,)), ((), ()))
TN = (((0,), (0,)), ((), ()))
SWAP = [(0, 1), (1, 0)]
BF16 = jnp.bfloat16
F32 = jnp.float32
IN_HBM = pl.BlockSpec(memory_space=pl.ANY)
IN_SMEM = pl.BlockSpec(memory_space=pltpu.SMEM)
IN_VMEM = pl.BlockSpec(memory_space=pltpu.VMEM)


def dot(a, b, dims):
    return lax.dot_general(a, b, dims, preferred_element_type=F32)


def near(value):
    return pltpu.with_memory_space_constraint(value, pltpu.VMEM)


def lanes(start, size):
    return pl.ds(pl.multiple_of(start, HD), size)


def call(kernel, in_specs, outs, operands, scratch=(), flops=0, exps=0, moved=1 << 20, room=4):
    out_specs = [IN_HBM if isinstance(o, jax.ShapeDtypeStruct) else IN_VMEM for o in outs]
    operands = [near(a) if spec is IN_VMEM else a for a, spec in zip(operands, in_specs)]
    return pl.pallas_call(
        kernel,
        in_specs=list(in_specs),
        out_specs=out_specs,
        out_shape=list(outs),
        scratch_shapes=list(scratch),
        cost_estimate=pl.CostEstimate(flops=flops, transcendentals=exps, bytes_accessed=moved),
        compiler_params=pltpu.CompilerParams(vmem_limit_bytes=room << 20),
    )(*operands)


def run_copies(copies):
    for copy in copies:
        copy.start()
    for copy in copies:
        copy.wait()


def pack_kernel(x_ref, out_ref, sems):
    run_copies(
        [
            pltpu.make_async_copy(
                x_ref.at[:, pl.ds((y * 4 + z) * FEAT, FEAT)], out_ref.at[z, y], sems.at[4 * z + y]
            )
            for z in range(4)
            for y in range(4)
        ]
    )


def pack(layer_input):
    return call(
        pack_kernel, [IN_HBM], [pltpu.VMEM((4, 4, BLK, FEAT), BF16)], [layer_input],
        [pltpu.SemaphoreType.DMA((16,))], moved=2 << 20,
    )[0]


def other_kernel(info, q_ref, do_ref, out_ref, sems):
    cols = lanes((1 - info[1]) * HALF, HALF)
    run_copies(
        [
            pltpu.make_async_copy(ref.at[:, cols], out_ref.at[i], sems.at[i])
            for i, ref in enumerate((q_ref, do_ref))
        ]
    )


def other_heads(info, queries, out_grad):
    return call(
        other_kernel, [IN_SMEM, IN_HBM, IN_HBM],
        [pltpu.VMEM((2, BLK, HALF), BF16)], [info, queries, out_grad],
        [pltpu.SemaphoreType.DMA((2,))], moved=1 << 20,
    )[0]


def side_parity(core, side):
    return core if side == 0 else 1 - core


def first_place(core, side, small):
    return 4 if small else side_parity(core, side)


def gather_keys(core, sources, which, start, buf):
    for j, kv in enumerate(sources):
        for side in range(2):
            buf[2 * j + side_parity(core, side)] = kv[side, which, :, lanes(start, HD)]


def write_bias(info, side, small, bias_ref):
    chip, core = info[0], info[1]
    win = 2 if small else WIN
    k_pos = (2 * chip - 4 + first_place(core, side, small)) * BLK + lax.broadcasted_iota(
        jnp.int32, (win * BLK, BLK), 0
    )
    lane = lax.broadcasted_iota(jnp.int32, (1, BLK), 1)
    q_pos = (2 * chip + side_parity(core, side)) * BLK + lane
    begin = jnp.zeros_like(q_pos)
    end = jnp.int32(0)
    for sample in range(8):
        end = end + info[2 + sample]
        begin = jnp.where(end <= q_pos, end, begin)
    allowed = (k_pos >= begin) & (k_pos <= q_pos)
    bias_ref[side, : win * BLK] = jnp.where(allowed, 0.0, MASKED)


def masked(raw, bias):
    return raw * EXP2_SCALE + jnp.concatenate([bias, bias], axis=1)


class Heads:
    def __init__(self, core, own_ref, oth_ref, which, group):
        self.own, self.oth, self.which = own_ref, oth_ref, which
        self.own_start = core * HALF + group * WIDTH
        self.oth_start = group * WIDTH

    def pair(self, side, pair):
        if side == 0:
            two = self.own[:, lanes(self.own_start + pair * COLS, COLS)]
        else:
            two = self.oth[self.which, :, lanes(self.oth_start + pair * COLS, COLS)]
        return jnp.concatenate([two[:, :HD], two[:, HD:]], axis=0)


def window_rows(core, side, small):
    return lanes(first_place(core, side, small) * BLK, (2 if small else WIN) * BLK)


def window(buf, core, side, small):
    win = 2 if small else WIN
    return buf[pl.ds(first_place(core, side, small), win)].reshape(win * BLK, HD)


def probs_body(small, core, group, q, do, k_buf, stat_ref, bias_ref, dv_acc):
    win = 2 if small else WIN

    def raw_scores(step):
        side, pair = divmod(step, PAIRS)
        return dot(window(k_buf, core, side, small), q.pair(side, pair), NT)

    following = raw_scores(0)
    for step in range(2 * PAIRS):
        side, pair = divmod(step, PAIRS)
        raw = following
        if step + 1 < 2 * PAIRS:
            following = raw_scores(step + 1)
        scores = masked(raw, bias_ref[side, : win * BLK])
        peak = jnp.max(scores, axis=0, keepdims=True)
        exponent = jnp.exp2(scores - peak)
        over = 1.0 / jnp.sum(exponent, axis=0, keepdims=True)
        stat_ref[group, 0, step : step + 1] = peak
        stat_ref[group, 1, step : step + 1] = over
        probs = (exponent * over).astype(BF16)
        dv_acc[window_rows(core, side, small), :] += dot(probs, do.pair(side, pair), NN)


def probs_kernel(
    info, q_own, do_own, others, kv_two, kv_one, kv_here,
    dv_two, dv_one, dv_here, stat_ref, bias_ref,
    k_buf, dv_acc,
):
    chip, core = info[0], info[1]
    for small in (True, False):
        @pl.when((chip == 0) == small)
        def _():
            for side in range(2):
                write_bias(info, side, small, bias_ref)

            def group_step(group, carry):
                gather_keys(core, (kv_two, kv_one, kv_here), 0, group * HD, k_buf)
                dv_acc[...] = jnp.zeros_like(dv_acc)
                q = Heads(core, q_own, others, 0, group)
                do = Heads(core, do_own, others, 1, group)
                probs_body(small, core, group, q, do, k_buf, stat_ref, bias_ref, dv_acc)
                for j, part in enumerate((dv_two, dv_one, dv_here)):
                    for side in range(2):
                        rows = lanes((2 * j + side_parity(core, side)) * BLK, BLK)
                        part[side, :, lanes(group * HD, HD)] = dv_acc[rows, :].astype(part.dtype)
                return carry

            lax.fori_loop(0, 2, group_step, 0)


def scores_body(small, core, q, do, k_buf, v_buf, k_t, stat_ref, bias_ref, dk_acc, dq_refs, at):
    win = 2 if small else WIN

    def products(step):
        side, pair = divmod(step, PAIRS)
        raw = dot(window(k_buf, core, side, small), q.pair(side, pair), NT)
        return raw, dot(window(v_buf, core, side, small), do.pair(side, pair), NT)

    following = products(0)
    for step in range(2 * PAIRS):
        side, pair = divmod(step, PAIRS)
        raw, dprobs = following
        if step + 1 < 2 * PAIRS:
            following = products(step + 1)
        rows = window_rows(core, side, small)
        peak, over = stat_ref[0, step : step + 1], stat_ref[1, step : step + 1]
        scores = masked(raw, bias_ref[side, : win * BLK])
        probs = jnp.exp2(scores - peak) * over
        delta = jnp.sum(probs * dprobs, axis=0, keepdims=True)
        dscores = (probs * (dprobs - delta)).astype(BF16)
        dk_acc[rows, :] += dot(dscores, q.pair(side, pair), NN)
        dq_t = dot(k_t[:, rows], dscores, NN) * SCALE
        for i in range(2):
            start = at + (2 * pair + i) * HD
            dq = dq_t[:, i * BLK : (i + 1) * BLK].T.astype(BF16)
            dq_refs[side][:, start : start + HD] = dq


def scores_kernel(group, info, q_own, do_own, others, kv_two, kv_one, kv_here, stat_ref, bias_ref, *refs):
    chip, core = info[0], info[1]
    if group == 0:
        dq_own, dq_oth, dk_acc, k_buf, v_buf, k_t = refs
    else:
        past_own, past_oth, past_dk, dq_own, dq_oth, dk_two, dk_one, dk_here = refs[:8]
        k_buf, v_buf, k_t, dk_acc = refs[8:]
        dq_own[:, :WIDTH] = past_own[...]
        dq_oth[:, :WIDTH] = past_oth[...]
    gather_keys(core, (kv_two, kv_one, kv_here), 0, group * HD, k_buf)
    gather_keys(core, (kv_two, kv_one, kv_here), 1, group * HD, v_buf)
    k_t[...] = k_buf[...].reshape(SPAN * BLK, HD).T
    dk_acc[...] = jnp.zeros_like(dk_acc)
    q = Heads(core, q_own, others, 0, group)
    do = Heads(core, do_own, others, 1, group)
    stat = stat_ref.at[group]
    for small in (True, False):
        @pl.when((chip == 0) == small)
        def _():
            scores_body(
                small, core, q, do, k_buf, v_buf, k_t, stat, bias_ref, dk_acc,
                (dq_own, dq_oth), group * WIDTH,
            )
    if group == 1:
        for j, part in enumerate((dk_two, dk_one, dk_here)):
            for side in range(2):
                rows = lanes((2 * j + side_parity(core, side)) * BLK, BLK)
                part[side, :, :HD] = (past_dk[rows, :] * SCALE).astype(part.dtype)
                part[side, :, HD:] = (dk_acc[rows, :] * SCALE).astype(part.dtype)


PARTS = [pltpu.VMEM((2, BLK, COLS), kind) for kind in (BF16, BF16, F32)]
KEYS = pltpu.VMEM((SPAN, BLK, HD), BF16)
TURNED = pltpu.VMEM((HD, SPAN * BLK), BF16)
TOTAL = pltpu.VMEM((SPAN * BLK, HD), F32)
PRODUCT = 2 * 16 * 2 * BLK * WIN * BLK * HD


def attention_probs(operands):
    stats = pltpu.VMEM((2, 2, 2 * PAIRS, 2 * BLK), F32)
    bias = pltpu.VMEM((2, WIN * BLK, BLK), F32)
    return call(
        probs_kernel, [IN_SMEM] + [IN_VMEM] * 6, PARTS + [stats, bias], operands,
        [KEYS, TOTAL], flops=2 * PRODUCT, exps=PRODUCT // 256, moved=4 << 20, room=16,
    )


def attention_scores(group, past, stats, bias, operands):
    def kernel(*refs):
        scores_kernel(group, *refs)

    wide = WIDTH * (group + 1)
    outs = [pltpu.VMEM((BLK, wide), BF16)] * 2 + ([TOTAL] if group == 0 else PARTS)
    scratch = [KEYS, KEYS, TURNED] + ([] if group == 0 else [TOTAL])
    return call(
        kernel, [IN_SMEM] + [IN_VMEM] * (8 + len(past)), outs,
        [*operands, stats, bias, *past], scratch,
        flops=2 * PRODUCT, exps=PRODUCT // 512, moved=4 << 20, room=16,
    )


def weight_kernel(info, x_own, x_oth, *refs):
    dv, out_ref = refs[:-1], refs[-1]
    z = info[2 + 8]
    sources = [lax.rem(z + 4 - back, 4) for back in range(4)]
    dv_rows = jnp.concatenate([dv[back][side] for back in range(4) for side in range(2)], axis=0)
    for y in range(4):
        x_rows = jnp.concatenate(
            [x[source, y] for source in sources for x in (x_own, x_oth)], axis=0
        )
        out_ref[y * FEAT : (y + 1) * FEAT] = dot(x_rows, dv_rows, TN).astype(BF16)


def weight_part(info, x_own, x_oth, dv):
    return call(
        weight_kernel, [IN_SMEM] + [IN_VMEM] * 6,
        [pltpu.VMEM((4 * FEAT, COLS), BF16)], [info, x_own, x_oth, *dv],
        flops=2 * 4 * FEAT * COLS * 8 * BLK, moved=6 << 20, room=16,
    )[0]


def weight_sum_kernel(got, out_ref):
    for side in range(2):
        total = got[side].astype(F32)
        for source in range(1, 16):
            total = total + got[2 * source + side].astype(F32)
        out_ref[:, side * COLS : (side + 1) * COLS] = total * (1.0 / math.sqrt(16 * LEN))


def weight_sum(got):
    return pl.pallas_call(
        weight_sum_kernel,
        in_specs=[IN_VMEM],
        out_specs=IN_VMEM,
        out_shape=jax.ShapeDtypeStruct((64, HK * HD), F32),
        compiler_params=pltpu.CompilerParams(vmem_limit_bytes=4 << 20),
        name="weight_sum",
    )(near(got))


def sum_kernel(here, one, two, out_ref):
    out_ref[...] = (here[...] + one[...].astype(F32) + two[...].astype(F32)).astype(BF16)


def part_sum(parts):
    return call(sum_kernel, [IN_VMEM] * 3, [pltpu.VMEM((2, BLK, COLS), BF16)], parts)[0]


def finish_kernel(info, dq_own, dq_got, dk, dv, got, query_grad, key_grad, value_grad, sems):
    core = info[1]
    keep, other = lanes(core * HALF, HALF), lanes((1 - core) * HALF, HALF)
    keep_kv, other_kv = lanes(core * COLS, COLS), lanes((1 - core) * COLS, COLS)
    moves = [
        (dq_own, query_grad.at[:, keep]),
        (dq_got, query_grad.at[:, other]),
        (dk.at[0], key_grad.at[:, keep_kv]),
        (got.at[0], key_grad.at[:, other_kv]),
        (dv.at[0], value_grad.at[:, keep_kv]),
        (got.at[1], value_grad.at[:, other_kv]),
    ]
    run_copies(
        [pltpu.make_async_copy(a, b, sems.at[i]) for i, (a, b) in enumerate(moves)]
    )


def finish(info, dq_own, dq_got, dk, dv, got):
    outs = [jax.ShapeDtypeStruct((BLK, width * HD), BF16) for width in (HQ, HK, HK)]
    return call(
        finish_kernel, [IN_SMEM] + [IN_VMEM] * 5, outs,
        [info, dq_own, dq_got, dk, dv, got], [pltpu.SemaphoreType.DMA((6,))], moved=2 << 20,
    )


def exchange(value, axes):
    return lax.all_to_all(value, axes, 0, 0, tiled=True)


def shards(queries, key_states, value_states, out_grad, layer_input, lengths):
    chip, core, depth = lax.axis_index("x"), lax.axis_index("core"), lax.axis_index("z")
    queries, out_grad = queries[0], out_grad[0]
    info = jnp.concatenate(
        [jnp.stack([chip, core]).astype(jnp.int32), lengths[0], depth.reshape(1).astype(jnp.int32)]
    )

    def pairs(a, b, which, width):
        cut = [lax.dynamic_slice(v, (0, which * width), (BLK, width)) for v in (a, b)]
        return jnp.stack(cut)

    kv_keep = pairs(key_states[0], value_states[0], core, COLS)
    kv_send = pairs(key_states[0], value_states[0], 1 - core, COLS)
    kv_here = jnp.stack([kv_keep, lax.ppermute(kv_send, "core", SWAP)])
    kv_two = lax.ppermute(kv_here, "x", [(0, 2), (1, 3)])
    kv_one = lax.ppermute(kv_here, "x", [(0, 1), (1, 2), (2, 3)])

    others = lax.ppermute(other_heads(info, queries, out_grad), "core", SWAP)

    x_own = exchange(pack(layer_input[0]), "z")
    x_oth = lax.ppermute(x_own, "core", SWAP)

    operands = (info, queries, out_grad, others, kv_two, kv_one, kv_here)
    dv_two, dv_one, dv_here, stats, bias = attention_probs(operands)
    past = ()
    for group in range(2):
        past = attention_scores(group, past, stats, bias, operands)
    dq_own, dq_oth, dk_two, dk_one, dk_here = past

    def summed(here, one, two):
        one = lax.ppermute(one, "x", [(1, 0), (2, 1), (3, 2)])
        two = lax.ppermute(two, "x", [(2, 0), (3, 1)])
        return part_sum([here, one, two])

    dv = summed(dv_here, dv_one, dv_two)
    dv_z = [dv] + [
        lax.ppermute(dv, "z", [(i, (i + away) % 4) for i in range(4)]) for away in (1, 2, 3)
    ]
    weight = weight_part(info, x_own, x_oth, dv_z)
    weight = weight_sum(exchange(weight.reshape(32, 64, COLS), ("y", "x", "core")))

    dk = summed(dk_here, dk_one, dk_two)
    dq_got = lax.ppermute(dq_oth, "core", SWAP)
    got = lax.ppermute(jnp.stack([dk[1], dv[1]]), "core", SWAP)
    query_grad, key_grad, value_grad = finish(info, dq_own, dq_got, dk, dv, got)
    return query_grad[None], key_grad[None], value_grad[None], weight


def solution(mesh):
    whole = Mesh(mesh.devices.reshape(4, 4, 4, 2), ("y", "z", "x", "core"))
    rows = P(("y", "z"), ("x", "core"), None)
    return jax.shard_map(
        shards,
        mesh=whole,
        in_specs=(rows,) * 5 + (P(("y", "z"), None),),
        out_specs=(rows,) * 3 + (P(("y", "z", "x", "core"), None),),
        check_vma=False,
    )
```

```python
import math

import jax
import jax.numpy as jnp
from jax import lax
from jax.experimental import pallas as pl
from jax.experimental.pallas import tpu as pltpu
from jax.sharding import Mesh, PartitionSpec as P


D = 8192
HQ = 32
HK = 4
HD = 128
LEN = 1024
BLK = 128
SPAN = 6
WIN = 5
GROUP = HQ // HK
PAIRS = GROUP // 2
WIDTH = GROUP * HD
HALF = HQ * HD // 2
COLS = 2 * HD
FEAT = D // 16
SCALE = HD ** (-0.5)
EXP2_SCALE = SCALE * math.log2(math.e)
MASKED = -1e30
NT = (((1,), (1,)), ((), ()))
NN = (((1,), (0,)), ((), ()))
TN = (((0,), (0,)), ((), ()))
SWAP = [(0, 1), (1, 0)]
BF16 = jnp.bfloat16
F32 = jnp.float32
IN_HBM = pl.BlockSpec(memory_space=pltpu.HBM)
IN_SMEM = pl.BlockSpec(memory_space=pltpu.SMEM)
IN_VMEM = pl.BlockSpec(memory_space=pltpu.VMEM)
ANYWHERE = pl.BlockSpec(memory_space=pltpu.VMEM)


def dot(a, b, dims):
    return lax.dot_general(a, b, dims, preferred_element_type=F32)


def near(value):
    return pltpu.with_memory_space_constraint(value, pltpu.VMEM)


def far(value):
    return pltpu.with_memory_space_constraint(value, pltpu.HBM)


def lanes(start, size):
    return pl.ds(pl.multiple_of(start, HD), size)


def call(kernel, in_specs, outs, operands, scratch=(), flops=0, exps=0, moved=1 << 20, room=4, aliases=None):
    out_specs = [IN_HBM if isinstance(o, jax.ShapeDtypeStruct) else IN_VMEM for o in outs]
    place = {id(IN_VMEM): near, id(IN_HBM): far}
    operands = [place.get(id(spec), lambda a: a)(a) for a, spec in zip(operands, in_specs)]
    return pl.pallas_call(
        kernel,
        in_specs=list(in_specs),
        out_specs=out_specs,
        out_shape=list(outs),
        scratch_shapes=list(scratch),
        cost_estimate=pl.CostEstimate(flops=flops, transcendentals=exps, bytes_accessed=moved),
        compiler_params=pltpu.CompilerParams(vmem_limit_bytes=room << 20),
        input_output_aliases=aliases or {},
    )(*operands)


def run_copies(copies):
    for copy in copies:
        copy.start()
    for copy in copies:
        copy.wait()


def pack_kernel(x_ref, out_ref, sems):
    run_copies(
        [
            pltpu.make_async_copy(
                x_ref.at[:, pl.ds((y * 4 + z) * FEAT, FEAT)], out_ref.at[z, y], sems.at[4 * z + y]
            )
            for z in range(4)
            for y in range(4)
        ]
    )


def pack(layer_input):
    return call(
        pack_kernel, [IN_HBM], [pltpu.VMEM((4, 4, BLK, FEAT), BF16)], [layer_input],
        [pltpu.SemaphoreType.DMA((16,))], moved=2 << 20,
    )[0]


def other_kernel(info, q_ref, do_ref, out_ref, sems):
    cols = lanes((1 - info[1]) * HALF, HALF)
    run_copies(
        [
            pltpu.make_async_copy(ref.at[:, cols], out_ref.at[i], sems.at[i])
            for i, ref in enumerate((q_ref, do_ref))
        ]
    )


def other_heads(info, queries, out_grad):
    return call(
        other_kernel, [IN_SMEM, IN_HBM, IN_HBM],
        [pltpu.VMEM((2, BLK, HALF), BF16)], [info, queries, out_grad],
        [pltpu.SemaphoreType.DMA((2,))], moved=1 << 20,
    )[0]


def side_parity(core, side):
    return core if side == 0 else 1 - core


def first_place(core, side, small):
    return 4 if small else side_parity(core, side)


def gather_keys(core, sources, which, group, buf):
    for j, kv in enumerate(sources):
        for side in range(2):
            place = 2 * j + side_parity(core, side)
            buf[group, place] = kv[side, which, :, group * HD : (group + 1) * HD]


def write_bias(info, side, small, bias_ref):
    chip, core = info[0], info[1]
    win = 2 if small else WIN
    k_pos = (2 * chip - 4 + first_place(core, side, small)) * BLK + lax.broadcasted_iota(
        jnp.int32, (win * BLK, BLK), 0
    )
    lane = lax.broadcasted_iota(jnp.int32, (1, BLK), 1)
    q_pos = (2 * chip + side_parity(core, side)) * BLK + lane
    begin = jnp.zeros_like(q_pos)
    end = jnp.int32(0)
    for sample in range(8):
        end = end + info[2 + sample]
        begin = jnp.where(end <= q_pos, end, begin)
    allowed = (k_pos >= begin) & (k_pos <= q_pos)
    bias_ref[side, : win * BLK] = jnp.where(allowed, 0.0, MASKED)


def masked(raw, bias):
    return raw * EXP2_SCALE + jnp.concatenate([bias, bias], axis=1)


def head_pair(own, oth, which, step):
    group, side, pair = place_of(step)
    start = group * WIDTH + pair * COLS
    two = (own if side == 0 else oth)[which, :, start : start + COLS]
    return jnp.concatenate([two[:, :HD], two[:, HD:]], axis=0)


STEPS = 4 * PAIRS


def place_of(step):
    group, rest = divmod(step, 2 * PAIRS)
    return group, 1 - rest // PAIRS, rest % PAIRS


def load_own(core, q_hbm, do_hbm, own, sems):
    cols = lanes(core * HALF, HALF)
    copies = [
        pltpu.make_async_copy(ref.at[:, cols], own.at[i], sems.at[i])
        for i, ref in enumerate((q_hbm, do_hbm))
    ]
    for copy in copies:
        copy.start()
    return copies


def window_rows(core, side, small):
    return lanes(first_place(core, side, small) * BLK, (2 if small else WIN) * BLK)


def window(buf, group, core, side, small):
    win = 2 if small else WIN
    return buf[group, pl.ds(first_place(core, side, small), win)].reshape(win * BLK, HD)


def store_parts(core, acc, parts, scale):
    for group in range(2):
        for j, part in enumerate(parts):
            for side in range(2):
                rows = lanes((2 * j + side_parity(core, side)) * BLK, BLK)
                cut = acc[group, rows, :]
                cut = cut if scale is None else cut * scale
                part[side, :, group * HD : (group + 1) * HD] = cut.astype(part.dtype)


def probs_body(small, core, own, others, loads, k_buf, stat_ref, bias_ref, dv_acc):
    win = 2 if small else WIN

    def raw_scores(step):
        if step == PAIRS:
            for load in loads:
                load.wait()
        group, side, _ = place_of(step)
        return dot(window(k_buf, group, core, side, small), head_pair(own, others, 0, step), NT)

    following = raw_scores(0)
    for step in range(STEPS):
        group, side, _ = place_of(step)
        raw = following
        if step + 1 < STEPS:
            following = raw_scores(step + 1)
        scores = masked(raw, bias_ref[side, : win * BLK])
        peak = jnp.max(scores, axis=0, keepdims=True)
        exponent = jnp.exp2(scores - peak)
        over = 1.0 / jnp.sum(exponent, axis=0, keepdims=True)
        stat_ref[0, step : step + 1] = peak
        stat_ref[1, step : step + 1] = over
        probs = (exponent * over).astype(BF16)
        dv_acc[group, window_rows(core, side, small), :] += dot(
            probs, head_pair(own, others, 1, step), NN
        )


def probs_kernel(
    info, q_hbm, do_hbm, others, kv_two, kv_one, kv_here,
    dv_two, dv_one, dv_here, stat_ref, bias_ref,
    k_buf, dv_acc, own, sems,
):
    chip, core = info[0], info[1]
    loads = load_own(core, q_hbm, do_hbm, own, sems)
    for group in range(2):
        gather_keys(core, (kv_two, kv_one, kv_here), 0, group, k_buf)
    dv_acc[...] = jnp.zeros_like(dv_acc)
    for small in (True, False):
        @pl.when((chip == 0) == small)
        def _():
            for side in range(2):
                write_bias(info, side, small, bias_ref)
            probs_body(small, core, own, others, loads, k_buf, stat_ref, bias_ref, dv_acc)
    store_parts(core, dv_acc, (dv_two, dv_one, dv_here), None)


def scores_body(
    small, core, own, others, loads, k_buf, v_buf, k_t, stat_ref, bias_ref, dk_acc, dq_buf
):
    win = 2 if small else WIN

    def products(step):
        if step == PAIRS:
            for load in loads:
                load.wait()
        group, side, _ = place_of(step)
        raw = dot(window(k_buf, group, core, side, small), head_pair(own, others, 0, step), NT)
        grad = dot(window(v_buf, group, core, side, small), head_pair(own, others, 1, step), NT)
        return raw, grad

    following = products(0)
    for step in range(STEPS):
        group, side, pair = place_of(step)
        raw, dprobs = following
        if step + 1 < STEPS:
            following = products(step + 1)
        rows = window_rows(core, side, small)
        peak, over = stat_ref[0, step : step + 1], stat_ref[1, step : step + 1]
        scores = masked(raw, bias_ref[side, : win * BLK])
        probs = jnp.exp2(scores - peak) * over
        delta = jnp.sum(probs * dprobs, axis=0, keepdims=True)
        dscores = (probs * (dprobs - delta)).astype(BF16)
        dk_acc[group, rows, :] += dot(dscores, head_pair(own, others, 0, step), NN)
        dq_t = dot(k_t[group, :, rows], dscores, NN) * SCALE
        for i in range(2):
            start = group * WIDTH + (2 * pair + i) * HD
            dq = dq_t[:, i * BLK : (i + 1) * BLK].T.astype(BF16)
            dq_buf[side, :, start : start + HD] = dq


def scores_kernel(
    info, q_hbm, do_hbm, others, kv_two, kv_one, kv_here, stat_ref, bias_ref,
    dq_hbm, sent_hbm, dk_two, dk_one, dk_here,
    k_buf, v_buf, k_t, dk_acc, own, sems, dq_buf, out_sems,
):
    chip, core = info[0], info[1]
    loads = load_own(core, q_hbm, do_hbm, own, sems)
    targets = (dq_hbm.at[:, lanes(core * HALF, HALF)], sent_hbm)
    stores = [
        pltpu.make_async_copy(dq_buf.at[side], target, out_sems.at[side])
        for side, target in enumerate(targets)
    ]
    for group in range(2):
        gather_keys(core, (kv_two, kv_one, kv_here), 0, group, k_buf)
        gather_keys(core, (kv_two, kv_one, kv_here), 1, group, v_buf)
        k_t[group] = k_buf[group].reshape(SPAN * BLK, HD).T
    dk_acc[...] = jnp.zeros_like(dk_acc)
    for small in (True, False):
        @pl.when((chip == 0) == small)
        def _():
            scores_body(
                small, core, own, others, loads, k_buf, v_buf, k_t, stat_ref, bias_ref, dk_acc,
                dq_buf,
            )
    for store in stores:
        store.start()
    store_parts(core, dk_acc, (dk_two, dk_one, dk_here), SCALE)
    for store in stores:
        store.wait()


PARTS = [pltpu.VMEM((2, BLK, COLS), kind) for kind in (BF16, BF16, F32)]
KEYS = pltpu.VMEM((2, SPAN, BLK, HD), BF16)
TURNED = pltpu.VMEM((2, HD, SPAN * BLK), BF16)
TOTAL = pltpu.VMEM((2, SPAN * BLK, HD), F32)
OWN = [pltpu.VMEM((2, BLK, HALF), BF16), pltpu.SemaphoreType.DMA((2,))]
PRODUCT = 2 * 16 * 2 * BLK * WIN * BLK * HD
OPERANDS = [IN_SMEM, IN_HBM, IN_HBM] + [IN_VMEM] * 4


def attention_probs(operands):
    stats = pltpu.VMEM((2, STEPS, 2 * BLK), F32)
    bias = pltpu.VMEM((2, WIN * BLK, BLK), F32)
    return call(
        probs_kernel, OPERANDS, PARTS + [stats, bias], operands,
        [KEYS, TOTAL] + OWN, flops=2 * PRODUCT, exps=PRODUCT // 256, moved=4 << 20, room=16,
    )


def attention_scores(operands, stats, bias):
    return call(
        scores_kernel, OPERANDS[:3] + [ANYWHERE] * 4 + [IN_VMEM] * 2,
        [jax.ShapeDtypeStruct((BLK, width), BF16) for width in (2 * HALF, HALF)] + PARTS,
        [*operands, stats, bias],
        [KEYS, KEYS, TURNED, TOTAL] + OWN
        + [pltpu.VMEM((2, BLK, HALF), BF16), pltpu.SemaphoreType.DMA((2,))],
        flops=4 * PRODUCT, exps=PRODUCT // 256, moved=4 << 20, room=16,
    )


def weight_kernel(info, x_own, x_oth, *refs):
    dv, out_ref = refs[:-1], refs[-1]
    z = info[2 + 8]
    sources = [lax.rem(z + 4 - back, 4) for back in range(4)]
    dv_rows = jnp.concatenate([dv[back][side] for back in range(4) for side in range(2)], axis=0)
    for y in range(4):
        x_rows = jnp.concatenate(
            [x[source, y] for source in sources for x in (x_own, x_oth)], axis=0
        )
        out_ref[y * FEAT : (y + 1) * FEAT] = dot(x_rows, dv_rows, TN).astype(BF16)


def weight_part(info, x_own, x_oth, dv):
    return call(
        weight_kernel, [IN_SMEM] + [IN_VMEM] * 6,
        [pltpu.VMEM((4 * FEAT, COLS), BF16)], [info, x_own, x_oth, *dv],
        flops=2 * 4 * FEAT * COLS * 8 * BLK, moved=6 << 20, room=16,
    )[0]


def weight_sum_kernel(got, out_ref):
    for side in range(2):
        total = got[side].astype(F32)
        for source in range(1, 16):
            total = total + got[2 * source + side].astype(F32)
        out_ref[:, side * COLS : (side + 1) * COLS] = total * (1.0 / math.sqrt(16 * LEN))


def weight_sum(got):
    return pl.pallas_call(
        weight_sum_kernel,
        in_specs=[IN_VMEM],
        out_specs=IN_VMEM,
        out_shape=jax.ShapeDtypeStruct((64, HK * HD), F32),
        compiler_params=pltpu.CompilerParams(vmem_limit_bytes=4 << 20),
        name="weight_sum",
    )(near(got))


def sum_kernel(here, one, two, out_ref):
    out_ref[...] = (here[...] + one[...].astype(F32) + two[...].astype(F32)).astype(BF16)


def part_sum(parts):
    return call(sum_kernel, [IN_VMEM] * 3, [pltpu.VMEM((2, BLK, COLS), BF16)], parts)[0]


def finish_kernel(info, dq_kept, dq_got, dk, dv, got, query_grad, key_grad, value_grad, sems):
    core = info[1]
    other = lanes((1 - core) * HALF, HALF)
    keep_kv, other_kv = lanes(core * COLS, COLS), lanes((1 - core) * COLS, COLS)
    moves = [
        (dq_got, query_grad.at[:, other]),
        (dk.at[0], key_grad.at[:, keep_kv]),
        (got.at[0], key_grad.at[:, other_kv]),
        (dv.at[0], value_grad.at[:, keep_kv]),
        (got.at[1], value_grad.at[:, other_kv]),
    ]
    run_copies(
        [pltpu.make_async_copy(a, b, sems.at[i]) for i, (a, b) in enumerate(moves)]
    )


def finish(info, dq_kept, dq_got, dk, dv, got):
    outs = [jax.ShapeDtypeStruct((BLK, width * HD), BF16) for width in (HQ, HK, HK)]
    return call(
        finish_kernel, [IN_SMEM, IN_HBM] + [ANYWHERE] * 4, outs,
        [info, dq_kept, dq_got, dk, dv, got], [pltpu.SemaphoreType.DMA((5,))], moved=2 << 20,
        aliases={1: 0},
    )


def exchange(value, axes):
    return lax.all_to_all(value, axes, 0, 0, tiled=True)


def shards(queries, key_states, value_states, out_grad, layer_input, lengths):
    chip, core, depth = lax.axis_index("x"), lax.axis_index("core"), lax.axis_index("z")
    queries, out_grad = queries[0], out_grad[0]
    info = jnp.concatenate(
        [jnp.stack([chip, core]).astype(jnp.int32), lengths[0], depth.reshape(1).astype(jnp.int32)]
    )

    def pairs(a, b, which, width):
        cut = [lax.dynamic_slice(v, (0, which * width), (BLK, width)) for v in (a, b)]
        return jnp.stack(cut)

    kv_keep = pairs(key_states[0], value_states[0], core, COLS)
    kv_send = pairs(key_states[0], value_states[0], 1 - core, COLS)
    kv_here = jnp.stack([kv_keep, lax.ppermute(kv_send, "core", SWAP)])
    kv_two = lax.ppermute(kv_here, "x", [(0, 2), (1, 3)])
    kv_one = lax.ppermute(kv_here, "x", [(0, 1), (1, 2), (2, 3)])

    others = lax.ppermute(other_heads(info, queries, out_grad), "core", SWAP)

    x_own = exchange(pack(layer_input[0]), "z")
    x_oth = lax.ppermute(x_own, "core", SWAP)

    operands = (info, queries, out_grad, others, kv_two, kv_one, kv_here)
    dv_two, dv_one, dv_here, stats, bias = attention_probs(operands)
    dq_kept, dq_sent, dk_two, dk_one, dk_here = attention_scores(operands, stats, bias)

    def summed(here, one, two):
        one = lax.ppermute(one, "x", [(1, 0), (2, 1), (3, 2)])
        two = lax.ppermute(two, "x", [(2, 0), (3, 1)])
        return part_sum([here, one, two])

    dv = summed(dv_here, dv_one, dv_two)
    dv_z = [dv] + [
        lax.ppermute(dv, "z", [(i, (i + away) % 4) for i in range(4)]) for away in (1, 2, 3)
    ]
    weight = weight_part(info, x_own, x_oth, dv_z)
    weight = weight_sum(exchange(weight.reshape(32, 64, COLS), ("y", "x", "core")))

    dk = summed(dk_here, dk_one, dk_two)
    dq_got = lax.ppermute(dq_sent, "core", SWAP)
    got = lax.ppermute(jnp.stack([dk[1], dv[1]]), "core", SWAP)
    query_grad, key_grad, value_grad = finish(info, dq_kept, dq_got, dk, dv, got)
    return query_grad[None], key_grad[None], value_grad[None], weight


def solution(mesh):
    whole = Mesh(mesh.devices.reshape(4, 4, 4, 2), ("y", "z", "x", "core"))
    rows = P(("y", "z"), ("x", "core"), None)
    return jax.shard_map(
        shards,
        mesh=whole,
        in_specs=(rows,) * 5 + (P(("y", "z"), None),),
        out_specs=(rows,) * 3 + (P(("y", "z", "x", "core"), None),),
        check_vma=False,
    )
```

```python
import math

import jax
import jax.numpy as jnp
from jax import lax
from jax.experimental import pallas as pl
from jax.experimental.pallas import tpu as pltpu
from jax.sharding import Mesh, PartitionSpec as P


D = 8192
HQ = 32
HK = 4
HD = 128
LEN = 1024
BLK = 128
SPAN = 6
WIN = 5
GROUP = HQ // HK
PAIRS = GROUP // 2
WIDTH = GROUP * HD
HALF = HQ * HD // 2
COLS = 2 * HD
FEAT = D // 16
SCALE = HD ** (-0.5)
EXP2_SCALE = SCALE * math.log2(math.e)
MASKED = -1e30
NT = (((1,), (1,)), ((), ()))
NN = (((1,), (0,)), ((), ()))
TN = (((0,), (0,)), ((), ()))
SWAP = [(0, 1), (1, 0)]
BF16 = jnp.bfloat16
F32 = jnp.float32
IN_HBM = pl.BlockSpec(memory_space=pltpu.HBM)
IN_SMEM = pl.BlockSpec(memory_space=pltpu.SMEM)
IN_VMEM = pl.BlockSpec(memory_space=pltpu.VMEM)
ANYWHERE = pl.BlockSpec(memory_space=pltpu.VMEM)


def dot(a, b, dims):
    return lax.dot_general(a, b, dims, preferred_element_type=F32)


def near(value):
    return pltpu.with_memory_space_constraint(value, pltpu.VMEM)


def far(value):
    return pltpu.with_memory_space_constraint(value, pltpu.HBM)


def lanes(start, size):
    return pl.ds(pl.multiple_of(start, HD), size)


def call(kernel, in_specs, outs, operands, scratch=(), flops=0, exps=0, moved=1 << 20, room=4, aliases=None):
    out_specs = [
        IN_HBM if getattr(o, "memory_space", None) != pltpu.VMEM else IN_VMEM for o in outs
    ]
    place = {id(IN_VMEM): near, id(IN_HBM): far}
    operands = [place.get(id(spec), lambda a: a)(a) for a, spec in zip(operands, in_specs)]
    return pl.pallas_call(
        kernel,
        in_specs=list(in_specs),
        out_specs=out_specs,
        out_shape=list(outs),
        scratch_shapes=list(scratch),
        cost_estimate=pl.CostEstimate(flops=flops, transcendentals=exps, bytes_accessed=moved),
        compiler_params=pltpu.CompilerParams(vmem_limit_bytes=room << 20),
        input_output_aliases=aliases or {},
    )(*operands)


def run_copies(copies):
    for copy in copies:
        copy.start()
    for copy in copies:
        copy.wait()


def pack_kernel(x_ref, out_ref, buf, load_sems, store_sems):
    loads, stores = [], []
    for z in range(4):
        for y in range(4):
            cols = pl.ds((y * 4 + z) * FEAT, FEAT)
            at = buf.at[z, y]
            loads.append(pltpu.make_async_copy(x_ref.at[:, cols], at, load_sems.at[4 * z + y]))
            stores.append(pltpu.make_async_copy(at, out_ref.at[z, y], store_sems.at[4 * z + y]))
    for load in loads:
        load.start()
    for load, store in zip(loads, stores):
        load.wait()
        store.start()
    for store in stores:
        store.wait()


def pack(layer_input):
    shape = (4, 4, BLK, FEAT)
    return call(
        pack_kernel, [IN_HBM], [pltpu.HBM(shape, BF16)], [layer_input],
        [pltpu.VMEM(shape, BF16)] + [pltpu.SemaphoreType.DMA((16,))] * 2, moved=4 << 20,
    )[0]


def other_kernel(q_ref, do_ref, out_ref, sems):
    cols = lanes((1 - lax.axis_index("core")) * HALF, HALF)
    run_copies(
        [
            pltpu.make_async_copy(ref.at[:, cols], out_ref.at[i], sems.at[i])
            for i, ref in enumerate((q_ref, do_ref))
        ]
    )


def other_heads(queries, out_grad):
    return call(
        other_kernel, [IN_HBM, IN_HBM],
        [pltpu.VMEM((2, BLK, HALF), BF16)], [queries, out_grad],
        [pltpu.SemaphoreType.DMA((2,))], moved=1 << 20,
    )[0]


def side_parity(core, side):
    return core if side == 0 else 1 - core


def first_place(core, side, small):
    return 4 if small else side_parity(core, side)


def gather_keys(core, sources, which, group, buf):
    for j, kv in enumerate(sources):
        for side in range(2):
            place = 2 * j + side_parity(core, side)
            buf[group, place] = kv[side, which, :, group * HD : (group + 1) * HD]


def write_bias(lengths, chip, core, side, small, bias_ref):
    win = 2 if small else WIN
    k_pos = (2 * chip - 4 + first_place(core, side, small)) * BLK + lax.broadcasted_iota(
        jnp.int32, (win * BLK, BLK), 0
    )
    lane = lax.broadcasted_iota(jnp.int32, (1, BLK), 1)
    q_pos = (2 * chip + side_parity(core, side)) * BLK + lane
    begin = jnp.zeros_like(q_pos)
    end = jnp.int32(0)
    for sample in range(8):
        end = end + lengths[0, sample]
        begin = jnp.where(end <= q_pos, end, begin)
    allowed = (k_pos >= begin) & (k_pos <= q_pos)
    bias_ref[side, : win * BLK] = jnp.where(allowed, 0.0, MASKED)


def masked(raw, bias):
    return raw * EXP2_SCALE + jnp.concatenate([bias, bias], axis=1)


def head_pair(own, oth, which, step):
    group, side, pair = place_of(step)
    start = group * WIDTH + pair * COLS
    two = (own if side == 0 else oth)[which, :, start : start + COLS]
    return jnp.concatenate([two[:, :HD], two[:, HD:]], axis=0)


STEPS = 4 * PAIRS


def place_of(step):
    group, rest = divmod(step, 2 * PAIRS)
    return group, 1 - rest // PAIRS, rest % PAIRS


def load_own(core, q_hbm, do_hbm, own, sems):
    cols = lanes(core * HALF, HALF)
    copies = [
        pltpu.make_async_copy(ref.at[:, cols], own.at[i], sems.at[i])
        for i, ref in enumerate((q_hbm, do_hbm))
    ]
    for copy in copies:
        copy.start()
    return copies


def window_rows(core, side, small):
    return lanes(first_place(core, side, small) * BLK, (2 if small else WIN) * BLK)


def window(buf, group, core, side, small):
    win = 2 if small else WIN
    return buf[group, pl.ds(first_place(core, side, small), win)].reshape(win * BLK, HD)


def store_parts(core, acc, parts, scale):
    for group in range(2):
        for j, part in enumerate(parts):
            for side in range(2):
                rows = lanes((2 * j + side_parity(core, side)) * BLK, BLK)
                cut = acc[group, rows, :]
                cut = cut if scale is None else cut * scale
                part[side, :, group * HD : (group + 1) * HD] = cut.astype(part.dtype)


def probs_body(small, core, own, others, loads, k_buf, stat_ref, bias_ref, dv_acc):
    win = 2 if small else WIN

    def raw_scores(step):
        if step == PAIRS:
            for load in loads:
                load.wait()
        group, side, _ = place_of(step)
        return dot(window(k_buf, group, core, side, small), head_pair(own, others, 0, step), NT)

    following = raw_scores(0)
    for step in range(STEPS):
        group, side, _ = place_of(step)
        raw = following
        if step + 1 < STEPS:
            following = raw_scores(step + 1)
        scores = masked(raw, bias_ref[side, : win * BLK])
        peak = jnp.max(scores, axis=0, keepdims=True)
        exponent = jnp.exp2(scores - peak)
        over = 1.0 / jnp.sum(exponent, axis=0, keepdims=True)
        stat_ref[0, step : step + 1] = peak
        stat_ref[1, step : step + 1] = over
        probs = (exponent * over).astype(BF16)
        dv_acc[group, window_rows(core, side, small), :] += dot(
            probs, head_pair(own, others, 1, step), NN
        )


def probs_kernel(
    lengths, q_hbm, do_hbm, others, kv_two, kv_one, kv_here,
    dv_two, dv_one, dv_here, stat_ref, bias_ref,
    k_buf, dv_acc, own, sems,
):
    chip, core = lax.axis_index("x"), lax.axis_index("core")
    loads = load_own(core, q_hbm, do_hbm, own, sems)
    for group in range(2):
        gather_keys(core, (kv_two, kv_one, kv_here), 0, group, k_buf)
    dv_acc[...] = jnp.zeros_like(dv_acc)
    for small in (True, False):
        @pl.when((chip == 0) == small)
        def _():
            for side in range(2):
                write_bias(lengths, chip, core, side, small, bias_ref)
            probs_body(small, core, own, others, loads, k_buf, stat_ref, bias_ref, dv_acc)
    store_parts(core, dv_acc, (dv_two, dv_one, dv_here), None)


def scores_body(
    small, core, own, others, loads, k_buf, v_buf, k_t, stat_ref, bias_ref, dk_acc, dq_refs
):
    win = 2 if small else WIN

    def products(step):
        if step == PAIRS:
            for load in loads:
                load.wait()
        group, side, _ = place_of(step)
        raw = dot(window(k_buf, group, core, side, small), head_pair(own, others, 0, step), NT)
        grad = dot(window(v_buf, group, core, side, small), head_pair(own, others, 1, step), NT)
        return raw, grad

    following = products(0)
    for step in range(STEPS):
        group, side, pair = place_of(step)
        raw, dprobs = following
        if step + 1 < STEPS:
            following = products(step + 1)
        rows = window_rows(core, side, small)
        peak, over = stat_ref[0, step : step + 1], stat_ref[1, step : step + 1]
        scores = masked(raw, bias_ref[side, : win * BLK])
        probs = jnp.exp2(scores - peak) * over
        delta = jnp.sum(probs * dprobs, axis=0, keepdims=True)
        dscores = (probs * (dprobs - delta)).astype(BF16)
        dk_acc[group, rows, :] += dot(dscores, head_pair(own, others, 0, step), NN)
        dq_t = dot(k_t[group, :, rows], dscores, NN) * SCALE
        for i in range(2):
            start = group * WIDTH + (2 * pair + i) * HD
            dq = dq_t[:, i * BLK : (i + 1) * BLK].T.astype(BF16)
            dq_refs[side][:, start : start + HD] = dq


def scores_kernel(
    lengths, q_hbm, do_hbm, others, kv_two, kv_one, kv_here, stat_ref, bias_ref,
    dq_hbm, dq_sent, dk_two, dk_one, dk_here,
    k_buf, v_buf, k_t, dk_acc, own, sems, dq_buf, out_sem,
):
    chip, core = lax.axis_index("x"), lax.axis_index("core")
    loads = load_own(core, q_hbm, do_hbm, own, sems)
    store = pltpu.make_async_copy(dq_buf, dq_hbm.at[:, lanes(core * HALF, HALF)], out_sem)
    for group in range(2):
        gather_keys(core, (kv_two, kv_one, kv_here), 0, group, k_buf)
        gather_keys(core, (kv_two, kv_one, kv_here), 1, group, v_buf)
        k_t[group] = k_buf[group].reshape(SPAN * BLK, HD).T
    dk_acc[...] = jnp.zeros_like(dk_acc)
    for small in (True, False):
        @pl.when((chip == 0) == small)
        def _():
            scores_body(
                small, core, own, others, loads, k_buf, v_buf, k_t, stat_ref, bias_ref, dk_acc,
                (dq_buf, dq_sent),
            )
    store.start()
    store_parts(core, dk_acc, (dk_two, dk_one, dk_here), SCALE)
    store.wait()


PARTS = [pltpu.VMEM((2, BLK, COLS), kind) for kind in (BF16, BF16, F32)]
KEYS = pltpu.VMEM((2, SPAN, BLK, HD), BF16)
TURNED = pltpu.VMEM((2, HD, SPAN * BLK), BF16)
TOTAL = pltpu.VMEM((2, SPAN * BLK, HD), F32)
OWN = [pltpu.VMEM((2, BLK, HALF), BF16), pltpu.SemaphoreType.DMA((2,))]
PRODUCT = 2 * 16 * 2 * BLK * WIN * BLK * HD
OPERANDS = [IN_SMEM, IN_HBM, IN_HBM] + [IN_VMEM] * 4


def attention_probs(operands):
    stats = pltpu.VMEM((2, STEPS, 2 * BLK), F32)
    bias = pltpu.VMEM((2, WIN * BLK, BLK), F32)
    return call(
        probs_kernel, OPERANDS, PARTS + [stats, bias], operands,
        [KEYS, TOTAL] + OWN, flops=2 * PRODUCT, exps=PRODUCT // 256, moved=4 << 20, room=16,
    )


def attention_scores(operands, stats, bias):
    return call(
        scores_kernel, OPERANDS[:3] + [ANYWHERE] * 4 + [IN_VMEM] * 2,
        [jax.ShapeDtypeStruct((BLK, 2 * HALF), BF16), pltpu.VMEM((BLK, HALF), BF16)] + PARTS,
        [*operands[:-1], far(operands[-1]), stats, bias],
        [KEYS, KEYS, TURNED, TOTAL] + OWN
        + [pltpu.VMEM((BLK, HALF), BF16), pltpu.SemaphoreType.DMA(())],
        flops=4 * PRODUCT, exps=PRODUCT // 256, moved=4 << 20, room=16,
    )


def weight_rows(z, x, dv, side, y):
    sources = [lax.rem(z + 4 - back, 4) for back in range(4)]
    x_rows = jnp.concatenate([x[source, y] for source in sources], axis=0)
    return dot(x_rows, jnp.concatenate([ref[side] for ref in dv], axis=0), TN)


def weight_own_kernel(x, *refs):
    z = lax.axis_index("z")
    for y in range(4):
        refs[-1][y * FEAT : (y + 1) * FEAT] = weight_rows(z, x, refs[:-1], 0, y)


def weight_all_kernel(x, past, *refs):
    z = lax.axis_index("z")
    for y in range(4):
        rows = slice(y * FEAT, (y + 1) * FEAT)
        refs[-1][rows] = (past[rows] + weight_rows(z, x, refs[:-1], 1, y)).astype(BF16)


def weight_part(x_own, x_oth, dv):
    flops = 4 * FEAT * COLS * 8 * BLK
    past = call(
        weight_own_kernel, [IN_VMEM] * 5, [pltpu.VMEM((4 * FEAT, COLS), F32)],
        [x_own, *dv], flops=flops, moved=4 << 20, room=12,
    )[0]
    return call(
        weight_all_kernel, [IN_VMEM] * 6, [pltpu.VMEM((4 * FEAT, COLS), BF16)],
        [x_oth, past, *dv], flops=flops, moved=4 << 20, room=12,
    )[0]


def weight_sum_kernel(got, out_ref):
    for side in range(2):
        total = got[side].astype(F32)
        for source in range(1, 16):
            total = total + got[2 * source + side].astype(F32)
        out_ref[:, side * COLS : (side + 1) * COLS] = total * (1.0 / math.sqrt(16 * LEN))


def weight_sum(got):
    return pl.pallas_call(
        weight_sum_kernel,
        in_specs=[IN_VMEM],
        out_specs=IN_VMEM,
        out_shape=jax.ShapeDtypeStruct((64, HK * HD), F32),
        compiler_params=pltpu.CompilerParams(vmem_limit_bytes=4 << 20),
        name="weight_sum",
    )(near(got))


def sum_kernel(here, one, two, out_ref):
    out_ref[...] = (here[...] + one[...].astype(F32) + two[...].astype(F32)).astype(BF16)


def part_sum(parts):
    return call(sum_kernel, [IN_VMEM] * 3, [pltpu.VMEM((2, BLK, COLS), BF16)], parts)[0]


def finish_kernel(dq_kept, dq_got, dk, dv, got, query_grad, key_grad, value_grad, sems):
    core = lax.axis_index("core")
    other = lanes((1 - core) * HALF, HALF)
    keep_kv, other_kv = lanes(core * COLS, COLS), lanes((1 - core) * COLS, COLS)
    moves = [
        (dq_got, query_grad.at[:, other]),
        (dk.at[0], key_grad.at[:, keep_kv]),
        (got.at[0], key_grad.at[:, other_kv]),
        (dv.at[0], value_grad.at[:, keep_kv]),
        (got.at[1], value_grad.at[:, other_kv]),
    ]
    run_copies(
        [pltpu.make_async_copy(a, b, sems.at[i]) for i, (a, b) in enumerate(moves)]
    )


def finish(dq_kept, dq_got, dk, dv, got):
    outs = [jax.ShapeDtypeStruct((BLK, width * HD), BF16) for width in (HQ, HK, HK)]
    return call(
        finish_kernel, [IN_HBM] + [ANYWHERE] * 4, outs,
        [dq_kept, dq_got, dk, dv, got], [pltpu.SemaphoreType.DMA((5,))], moved=2 << 20,
        aliases={0: 0},
    )


def exchange(value, axes):
    return lax.all_to_all(value, axes, 0, 0, tiled=True)


def shards(queries, key_states, value_states, out_grad, layer_input, lengths):
    core = lax.axis_index("core")
    queries, out_grad = queries[0], out_grad[0]

    def pairs(a, b, which, width):
        cut = [lax.dynamic_slice(v, (0, which * width), (BLK, width)) for v in (a, b)]
        return jnp.stack(cut)

    kv_keep = pairs(key_states[0], value_states[0], core, COLS)
    kv_send = pairs(key_states[0], value_states[0], 1 - core, COLS)
    kv_here = jnp.stack([kv_keep, lax.ppermute(kv_send, "core", SWAP)])
    kv_two = lax.ppermute(kv_here, "x", [(0, 2), (1, 3)])
    kv_one = lax.ppermute(kv_here, "x", [(0, 1), (1, 2), (2, 3)])

    others = lax.ppermute(other_heads(queries, out_grad), "core", SWAP)

    x_own = exchange(pack(layer_input[0]), "z")
    x_oth = lax.ppermute(x_own, "core", SWAP)

    operands = (lengths, queries, out_grad, others, kv_two, kv_one, kv_here)
    dv_two, dv_one, dv_here, stats, bias = attention_probs(operands)
    dq_kept, dq_sent, dk_two, dk_one, dk_here = attention_scores(operands, stats, bias)

    def summed(here, one, two):
        one = lax.ppermute(one, "x", [(1, 0), (2, 1), (3, 2)])
        two = lax.ppermute(two, "x", [(2, 0), (3, 1)])
        return part_sum([here, one, two])

    dv = summed(dv_here, dv_one, dv_two)
    dv_z = [dv] + [
        lax.ppermute(dv, "z", [(i, (i + away) % 4) for i in range(4)]) for away in (1, 2, 3)
    ]
    weight = weight_part(x_own, x_oth, dv_z)
    weight = weight_sum(exchange(weight.reshape(32, 64, COLS), ("y", "x", "core")))

    dk = summed(dk_here, dk_one, dk_two)
    dq_got = lax.ppermute(dq_sent, "core", SWAP)
    got = lax.ppermute(jnp.stack([dk[1], dv[1]]), "core", SWAP)
    query_grad, key_grad, value_grad = finish(dq_kept, dq_got, dk, dv, got)
    return query_grad[None], key_grad[None], value_grad[None], weight


def solution(mesh):
    whole = Mesh(mesh.devices.reshape(4, 4, 4, 2), ("y", "z", "x", "core"))
    rows = P(("y", "z"), ("x", "core"), None)
    return jax.shard_map(
        shards,
        mesh=whole,
        in_specs=(rows,) * 5 + (P(("y", "z"), None),),
        out_specs=(rows,) * 3 + (P(("y", "z", "x", "core"), None),),
        check_vma=False,
    )
```

```python
import math

import jax
import jax.numpy as jnp
from jax import lax
from jax.experimental import pallas as pl
from jax.experimental.pallas import tpu as pltpu
from jax.sharding import Mesh, PartitionSpec as P


D = 8192
HQ = 32
HK = 4
HD = 128
LEN = 1024
BLK = 128
SPAN = 6
WIN = 5
GROUP = HQ // HK
PAIRS = GROUP // 2
WIDTH = GROUP * HD
HALF = HQ * HD // 2
COLS = 2 * HD
FEAT = D // 16
SCALE = HD ** (-0.5)
EXP2_SCALE = SCALE * math.log2(math.e)
MASKED = -1e30
NT = (((1,), (1,)), ((), ()))
NN = (((1,), (0,)), ((), ()))
TN = (((0,), (0,)), ((), ()))
SWAP = [(0, 1), (1, 0)]
BF16 = jnp.bfloat16
F32 = jnp.float32
IN_HBM = pl.BlockSpec(memory_space=pltpu.HBM)
IN_SMEM = pl.BlockSpec(memory_space=pltpu.SMEM)
IN_VMEM = pl.BlockSpec(memory_space=pltpu.VMEM)
ANYWHERE = pl.BlockSpec(memory_space=pltpu.VMEM)


def dot(a, b, dims):
    return lax.dot_general(a, b, dims, preferred_element_type=F32)


def near(value):
    return pltpu.with_memory_space_constraint(value, pltpu.VMEM)


def far(value):
    return pltpu.with_memory_space_constraint(value, pltpu.HBM)


def lanes(start, size):
    return pl.ds(pl.multiple_of(start, HD), size)


def call(kernel, in_specs, outs, operands, scratch=(), flops=0, exps=0, moved=1 << 20, room=4, aliases=None):
    out_specs = [
        IN_HBM if getattr(o, "memory_space", None) != pltpu.VMEM else IN_VMEM for o in outs
    ]
    place = {id(IN_VMEM): near, id(IN_HBM): far}
    operands = [place.get(id(spec), lambda a: a)(a) for a, spec in zip(operands, in_specs)]
    return pl.pallas_call(
        kernel,
        in_specs=list(in_specs),
        out_specs=out_specs,
        out_shape=list(outs),
        scratch_shapes=list(scratch),
        cost_estimate=pl.CostEstimate(flops=flops, transcendentals=exps, bytes_accessed=moved),
        compiler_params=pltpu.CompilerParams(vmem_limit_bytes=room << 20),
        input_output_aliases=aliases or {},
    )(*operands)


def run_copies(copies):
    for copy in copies:
        copy.start()
    for copy in copies:
        copy.wait()


def pack_kernel(x_ref, out_ref, buf, load_sems, store_sems):
    loads, stores = [], []
    for z in range(4):
        for y in range(4):
            cols = pl.ds((y * 4 + z) * FEAT, FEAT)
            at = buf.at[z, y]
            loads.append(pltpu.make_async_copy(x_ref.at[:, cols], at, load_sems.at[4 * z + y]))
            stores.append(pltpu.make_async_copy(at, out_ref.at[z, y], store_sems.at[4 * z + y]))
    for load in loads:
        load.start()
    for load, store in zip(loads, stores):
        load.wait()
        store.start()
    for store in stores:
        store.wait()


def pack(layer_input):
    shape = (4, 4, BLK, FEAT)
    return call(
        pack_kernel, [IN_HBM], [pltpu.HBM(shape, BF16)], [layer_input],
        [pltpu.VMEM(shape, BF16)] + [pltpu.SemaphoreType.DMA((16,))] * 2, moved=4 << 20,
    )[0]


def other_kernel(q_ref, do_ref, out_ref, sems):
    cols = lanes((1 - lax.axis_index("core")) * HALF, HALF)
    run_copies(
        [
            pltpu.make_async_copy(ref.at[:, cols], out_ref.at[i], sems.at[i])
            for i, ref in enumerate((q_ref, do_ref))
        ]
    )


def other_heads(queries, out_grad):
    return call(
        other_kernel, [IN_HBM, IN_HBM],
        [pltpu.VMEM((2, BLK, HALF), BF16)], [queries, out_grad],
        [pltpu.SemaphoreType.DMA((2,))], moved=1 << 20,
    )[0]


def side_parity(core, side):
    return core if side == 0 else 1 - core


def first_place(core, side, small):
    return 4 if small else side_parity(core, side)


def gather_keys(core, sources, which, group, buf):
    for j, kv in enumerate(sources):
        for side in range(2):
            place = 2 * j + side_parity(core, side)
            buf[group, place] = kv[side, which, :, group * HD : (group + 1) * HD]


def write_bias(lengths, chip, core, side, small, bias_ref):
    win = 2 if small else WIN
    k_pos = (2 * chip - 4 + first_place(core, side, small)) * BLK + lax.broadcasted_iota(
        jnp.int32, (win * BLK, BLK), 0
    )
    lane = lax.broadcasted_iota(jnp.int32, (1, BLK), 1)
    q_pos = (2 * chip + side_parity(core, side)) * BLK + lane
    begin = jnp.zeros_like(q_pos)
    end = jnp.int32(0)
    for sample in range(8):
        end = end + lengths[0, sample]
        begin = jnp.where(end <= q_pos, end, begin)
    allowed = (k_pos >= begin) & (k_pos <= q_pos)
    bias_ref[side, : win * BLK] = jnp.where(allowed, 0.0, MASKED)


def masked(raw, bias):
    return raw * EXP2_SCALE + jnp.concatenate([bias, bias], axis=1)


def head_pair(own, oth, which, step):
    group, side, pair = place_of(step)
    start = group * WIDTH + pair * COLS
    two = (own if side == 0 else oth)[which, :, start : start + COLS]
    return jnp.concatenate([two[:, :HD], two[:, HD:]], axis=0)


STEPS = 4 * PAIRS


def place_of(step):
    group, rest = divmod(step, 2 * PAIRS)
    return group, 1 - rest // PAIRS, rest % PAIRS


def load_own(core, q_hbm, do_hbm, own, sems):
    cols = lanes(core * HALF, HALF)
    copies = [
        pltpu.make_async_copy(ref.at[:, cols], own.at[i], sems.at[i])
        for i, ref in enumerate((q_hbm, do_hbm))
    ]
    for copy in copies:
        copy.start()
    return copies


def window_rows(core, side, small):
    return lanes(first_place(core, side, small) * BLK, (2 if small else WIN) * BLK)


def window(buf, group, core, side, small):
    win = 2 if small else WIN
    return buf[group, pl.ds(first_place(core, side, small), win)].reshape(win * BLK, HD)


def store_parts(core, acc, parts, scale):
    for group in range(2):
        for j, part in enumerate(parts):
            for side in range(2):
                rows = lanes((2 * j + side_parity(core, side)) * BLK, BLK)
                cut = acc[group, rows, :]
                cut = cut if scale is None else cut * scale
                part[side, :, group * HD : (group + 1) * HD] = cut.astype(part.dtype)


def probs_body(small, core, own, others, loads, k_buf, stat_ref, bias_ref, dv_acc):
    win = 2 if small else WIN

    def raw_scores(step):
        if step == PAIRS:
            for load in loads:
                load.wait()
        group, side, _ = place_of(step)
        return dot(window(k_buf, group, core, side, small), head_pair(own, others, 0, step), NT)

    following = raw_scores(0)
    for step in range(STEPS):
        group, side, _ = place_of(step)
        raw = following
        if step + 1 < STEPS:
            following = raw_scores(step + 1)
        scores = masked(raw, bias_ref[side, : win * BLK])
        peak = jnp.max(scores, axis=0, keepdims=True)
        exponent = jnp.exp2(scores - peak)
        over = 1.0 / jnp.sum(exponent, axis=0, keepdims=True)
        stat_ref[0, step : step + 1] = peak
        stat_ref[1, step : step + 1] = over
        probs = (exponent * over).astype(BF16)
        dv_acc[group, window_rows(core, side, small), :] += dot(
            probs, head_pair(own, others, 1, step), NN
        )


def probs_kernel(
    lengths, q_hbm, do_hbm, others, kv_two, kv_one, kv_here,
    dv_two, dv_one, dv_here, stat_ref, bias_ref,
    k_buf, dv_acc, own, sems,
):
    chip, core = lax.axis_index("x"), lax.axis_index("core")
    loads = load_own(core, q_hbm, do_hbm, own, sems)
    for group in range(2):
        gather_keys(core, (kv_two, kv_one, kv_here), 0, group, k_buf)
    dv_acc[...] = jnp.zeros_like(dv_acc)
    for small in (True, False):
        @pl.when((chip == 0) == small)
        def _():
            for side in range(2):
                write_bias(lengths, chip, core, side, small, bias_ref)
            probs_body(small, core, own, others, loads, k_buf, stat_ref, bias_ref, dv_acc)
    store_parts(core, dv_acc, (dv_two, dv_one, dv_here), None)


def scores_body(
    small, core, own, others, loads, k_buf, v_buf, k_t, stat_ref, bias_ref, dk_acc, dq_buf
):
    win = 2 if small else WIN

    def products(step):
        if step == PAIRS:
            for load in loads:
                load.wait()
        group, side, _ = place_of(step)
        raw = dot(window(k_buf, group, core, side, small), head_pair(own, others, 0, step), NT)
        grad = dot(window(v_buf, group, core, side, small), head_pair(own, others, 1, step), NT)
        return raw, grad

    following = products(0)
    for step in range(STEPS):
        group, side, pair = place_of(step)
        raw, dprobs = following
        if step + 1 < STEPS:
            following = products(step + 1)
        rows = window_rows(core, side, small)
        peak, over = stat_ref[0, step : step + 1], stat_ref[1, step : step + 1]
        scores = masked(raw, bias_ref[side, : win * BLK])
        probs = jnp.exp2(scores - peak) * over
        delta = jnp.sum(probs * dprobs, axis=0, keepdims=True)
        dscores = (probs * (dprobs - delta)).astype(BF16)
        dk_acc[group, rows, :] += dot(dscores, head_pair(own, others, 0, step), NN)
        dq_t = dot(k_t[group, :, rows], dscores, NN) * SCALE
        for i in range(2):
            start = group * WIDTH + (2 * pair + i) * HD
            dq = dq_t[:, i * BLK : (i + 1) * BLK].T.astype(BF16)
            dq_buf[side, :, start : start + HD] = dq


def scores_kernel(
    lengths, q_hbm, do_hbm, others, kv_two, kv_one, kv_here, stat_ref, bias_ref,
    dq_hbm, sent_hbm, dk_two, dk_one, dk_here,
    k_buf, v_buf, k_t, dk_acc, own, sems, dq_buf, out_sems,
):
    chip, core = lax.axis_index("x"), lax.axis_index("core")
    loads = load_own(core, q_hbm, do_hbm, own, sems)
    targets = (dq_hbm.at[:, lanes(core * HALF, HALF)], sent_hbm)
    stores = [
        pltpu.make_async_copy(dq_buf.at[side], target, out_sems.at[side])
        for side, target in enumerate(targets)
    ]
    for group in range(2):
        gather_keys(core, (kv_two, kv_one, kv_here), 0, group, k_buf)
        gather_keys(core, (kv_two, kv_one, kv_here), 1, group, v_buf)
        k_t[group] = k_buf[group].reshape(SPAN * BLK, HD).T
    dk_acc[...] = jnp.zeros_like(dk_acc)
    for small in (True, False):
        @pl.when((chip == 0) == small)
        def _():
            scores_body(
                small, core, own, others, loads, k_buf, v_buf, k_t, stat_ref, bias_ref, dk_acc,
                dq_buf,
            )
    for store in stores:
        store.start()
    store_parts(core, dk_acc, (dk_two, dk_one, dk_here), SCALE)
    for store in stores:
        store.wait()


PARTS = [pltpu.VMEM((2, BLK, COLS), kind) for kind in (BF16, BF16, F32)]
KEYS = pltpu.VMEM((2, SPAN, BLK, HD), BF16)
TURNED = pltpu.VMEM((2, HD, SPAN * BLK), BF16)
TOTAL = pltpu.VMEM((2, SPAN * BLK, HD), F32)
OWN = [pltpu.VMEM((2, BLK, HALF), BF16), pltpu.SemaphoreType.DMA((2,))]
PRODUCT = 2 * 16 * 2 * BLK * WIN * BLK * HD
OPERANDS = [IN_SMEM, IN_HBM, IN_HBM] + [IN_VMEM] * 4


def attention_probs(operands):
    stats = pltpu.VMEM((2, STEPS, 2 * BLK), F32)
    bias = pltpu.VMEM((2, WIN * BLK, BLK), F32)
    return call(
        probs_kernel, OPERANDS, PARTS + [stats, bias], operands,
        [KEYS, TOTAL] + OWN, flops=2 * PRODUCT, exps=PRODUCT // 256, moved=4 << 20, room=16,
    )


def attention_scores(operands, stats, bias):
    return call(
        scores_kernel, OPERANDS[:3] + [ANYWHERE] * 4 + [IN_VMEM] * 2,
        [pltpu.HBM((BLK, width), BF16) for width in (2 * HALF, HALF)] + PARTS,
        [*operands[:-1], far(operands[-1]), stats, bias],
        [KEYS, KEYS, TURNED, TOTAL] + OWN
        + [pltpu.VMEM((2, BLK, HALF), BF16), pltpu.SemaphoreType.DMA((2,))],
        flops=4 * PRODUCT, exps=PRODUCT // 256, moved=4 << 20, room=16,
    )


def weight_rows(z, x, dv, side, y):
    sources = [lax.rem(z + 4 - back, 4) for back in range(4)]
    x_rows = jnp.concatenate([x[source, y] for source in sources], axis=0)
    return dot(x_rows, jnp.concatenate([ref[side] for ref in dv], axis=0), TN)


def weight_own_kernel(x, *refs):
    z = lax.axis_index("z")
    for y in range(4):
        refs[-1][y * FEAT : (y + 1) * FEAT] = weight_rows(z, x, refs[:-1], 0, y)


def weight_all_kernel(x, past, *refs):
    z = lax.axis_index("z")
    for y in range(4):
        rows = slice(y * FEAT, (y + 1) * FEAT)
        refs[-1][rows] = (past[rows] + weight_rows(z, x, refs[:-1], 1, y)).astype(BF16)


def weight_part(x_own, x_oth, dv):
    flops = 4 * FEAT * COLS * 8 * BLK
    past = call(
        weight_own_kernel, [IN_VMEM] * 5, [pltpu.VMEM((4 * FEAT, COLS), F32)],
        [x_own, *dv], flops=flops, moved=4 << 20, room=12,
    )[0]
    return call(
        weight_all_kernel, [IN_VMEM] * 6, [pltpu.VMEM((4 * FEAT, COLS), BF16)],
        [x_oth, past, *dv], flops=flops, moved=4 << 20, room=12,
    )[0]


def weight_sum_kernel(got, out_ref):
    for side in range(2):
        total = got[side].astype(F32)
        for source in range(1, 16):
            total = total + got[2 * source + side].astype(F32)
        out_ref[:, side * COLS : (side + 1) * COLS] = total * (1.0 / math.sqrt(16 * LEN))


def weight_sum(got):
    return pl.pallas_call(
        weight_sum_kernel,
        in_specs=[IN_VMEM],
        out_specs=IN_VMEM,
        out_shape=jax.ShapeDtypeStruct((64, HK * HD), F32),
        compiler_params=pltpu.CompilerParams(vmem_limit_bytes=4 << 20),
        name="weight_sum",
    )(near(got))


def sum_kernel(here, one, two, out_ref):
    out_ref[...] = (here[...] + one[...].astype(F32) + two[...].astype(F32)).astype(BF16)


def part_sum(parts):
    return call(sum_kernel, [IN_VMEM] * 3, [pltpu.VMEM((2, BLK, COLS), BF16)], parts)[0]


def finish_kernel(dq_kept, dq_got, dk, dv, got, query_grad, key_grad, value_grad, sems):
    core = lax.axis_index("core")
    other = lanes((1 - core) * HALF, HALF)
    keep_kv, other_kv = lanes(core * COLS, COLS), lanes((1 - core) * COLS, COLS)
    moves = [
        (dq_got, query_grad.at[:, other]),
        (dk.at[0], key_grad.at[:, keep_kv]),
        (got.at[0], key_grad.at[:, other_kv]),
        (dv.at[0], value_grad.at[:, keep_kv]),
        (got.at[1], value_grad.at[:, other_kv]),
    ]
    run_copies(
        [pltpu.make_async_copy(a, b, sems.at[i]) for i, (a, b) in enumerate(moves)]
    )


def finish(dq_kept, dq_got, dk, dv, got):
    outs = [jax.ShapeDtypeStruct((BLK, width * HD), BF16) for width in (HQ, HK, HK)]
    return call(
        finish_kernel, [IN_HBM] + [ANYWHERE] * 4, outs,
        [dq_kept, dq_got, dk, dv, got], [pltpu.SemaphoreType.DMA((5,))], moved=2 << 20,
        aliases={0: 0},
    )


def exchange(value, axes):
    return lax.all_to_all(value, axes, 0, 0, tiled=True)


def shards(queries, key_states, value_states, out_grad, layer_input, lengths):
    core = lax.axis_index("core")
    queries, out_grad = queries[0], out_grad[0]

    def pairs(a, b, which, width):
        cut = [lax.dynamic_slice(v, (0, which * width), (BLK, width)) for v in (a, b)]
        return jnp.stack(cut)

    kv_keep = pairs(key_states[0], value_states[0], core, COLS)
    kv_send = pairs(key_states[0], value_states[0], 1 - core, COLS)
    kv_here = jnp.stack([kv_keep, lax.ppermute(kv_send, "core", SWAP)])
    kv_two = lax.ppermute(kv_here, "x", [(0, 2), (1, 3)])
    kv_one = lax.ppermute(kv_here, "x", [(0, 1), (1, 2), (2, 3)])

    others = lax.ppermute(other_heads(queries, out_grad), "core", SWAP)

    x_own = exchange(pack(layer_input[0]), "z")
    x_oth = lax.ppermute(x_own, "core", SWAP)

    operands = (lengths, queries, out_grad, others, kv_two, kv_one, kv_here)
    dv_two, dv_one, dv_here, stats, bias = attention_probs(operands)
    dq_kept, dq_sent, dk_two, dk_one, dk_here = attention_scores(operands, stats, bias)

    def summed(here, one, two):
        one = lax.ppermute(one, "x", [(1, 0), (2, 1), (3, 2)])
        two = lax.ppermute(two, "x", [(2, 0), (3, 1)])
        return part_sum([here, one, two])

    dv = summed(dv_here, dv_one, dv_two)
    dv_z = [dv] + [
        lax.ppermute(dv, "z", [(i, (i + away) % 4) for i in range(4)]) for away in (1, 2, 3)
    ]
    weight = weight_part(x_own, x_oth, dv_z)
    weight = weight_sum(exchange(weight.reshape(32, 64, COLS), ("y", "x", "core")))

    dk = summed(dk_here, dk_one, dk_two)
    dq_got = lax.ppermute(dq_sent, "core", SWAP)
    got = lax.ppermute(jnp.stack([dk[1], dv[1]]), "core", SWAP)
    query_grad, key_grad, value_grad = finish(dq_kept, dq_got, dk, dv, got)
    return query_grad[None], key_grad[None], value_grad[None], weight


def solution(mesh):
    whole = Mesh(mesh.devices.reshape(4, 4, 4, 2), ("y", "z", "x", "core"))
    rows = P(("y", "z"), ("x", "core"), None)
    return jax.shard_map(
        shards,
        mesh=whole,
        in_specs=(rows,) * 5 + (P(("y", "z"), None),),
        out_specs=(rows,) * 3 + (P(("y", "z", "x", "core"), None),),
        check_vma=False,
    )
```

```python
import math

import jax
import jax.numpy as jnp
from jax import lax
from jax.experimental import pallas as pl
from jax.experimental.pallas import tpu as pltpu
from jax.sharding import Mesh, PartitionSpec as P


D = 8192
HQ = 32
HK = 4
HD = 128
LEN = 1024
BLK = 128
SPAN = 6
WIN = 5
GROUP = HQ // HK
PAIRS = GROUP // 2
WIDTH = GROUP * HD
HALF = HQ * HD // 2
COLS = 2 * HD
FEAT = D // 16
SCALE = HD ** (-0.5)
EXP2_SCALE = SCALE * math.log2(math.e)
MASKED = -1e30
NT = (((1,), (1,)), ((), ()))
NN = (((1,), (0,)), ((), ()))
TN = (((0,), (0,)), ((), ()))
SWAP = [(0, 1), (1, 0)]
BF16 = jnp.bfloat16
F32 = jnp.float32
IN_HBM = pl.BlockSpec(memory_space=pltpu.HBM)
IN_SMEM = pl.BlockSpec(memory_space=pltpu.SMEM)
IN_VMEM = pl.BlockSpec(memory_space=pltpu.VMEM)
ANYWHERE = pl.BlockSpec(memory_space=pltpu.VMEM)


def dot(a, b, dims):
    return lax.dot_general(a, b, dims, preferred_element_type=F32)


def near(value):
    return pltpu.with_memory_space_constraint(value, pltpu.VMEM)


def far(value):
    return pltpu.with_memory_space_constraint(value, pltpu.HBM)


def lanes(start, size):
    return pl.ds(pl.multiple_of(start, HD), size)


def call(kernel, in_specs, outs, operands, scratch=(), flops=0, exps=0, moved=1 << 20, room=4, aliases=None):
    out_specs = [
        IN_HBM if getattr(o, "memory_space", None) != pltpu.VMEM else IN_VMEM for o in outs
    ]
    place = {id(IN_VMEM): near, id(IN_HBM): far}
    operands = [place.get(id(spec), lambda a: a)(a) for a, spec in zip(operands, in_specs)]
    return pl.pallas_call(
        kernel,
        in_specs=list(in_specs),
        out_specs=out_specs,
        out_shape=list(outs),
        scratch_shapes=list(scratch),
        cost_estimate=pl.CostEstimate(flops=flops, transcendentals=exps, bytes_accessed=moved),
        compiler_params=pltpu.CompilerParams(vmem_limit_bytes=room << 20),
        input_output_aliases=aliases or {},
    )(*operands)


def run_copies(copies):
    for copy in copies:
        copy.start()
    for copy in copies:
        copy.wait()


def pack_kernel(x_ref, out_ref, buf, load_sems, store_sems):
    loads, stores = [], []
    for z in range(4):
        for y in range(4):
            cols = pl.ds((y * 4 + z) * FEAT, FEAT)
            at = buf.at[z, y]
            loads.append(pltpu.make_async_copy(x_ref.at[:, cols], at, load_sems.at[4 * z + y]))
            stores.append(pltpu.make_async_copy(at, out_ref.at[z, y], store_sems.at[4 * z + y]))
    for load in loads:
        load.start()
    for load, store in zip(loads, stores):
        load.wait()
        store.start()
    for store in stores:
        store.wait()


def pack(layer_input):
    shape = (4, 4, BLK, FEAT)
    return call(
        pack_kernel, [IN_HBM], [pltpu.HBM(shape, BF16)], [layer_input],
        [pltpu.VMEM(shape, BF16)] + [pltpu.SemaphoreType.DMA((16,))] * 2, moved=4 << 20,
    )[0]


def other_kernel(q_ref, do_ref, out_ref, sems):
    cols = lanes((1 - lax.axis_index("core")) * HALF, HALF)
    run_copies(
        [
            pltpu.make_async_copy(ref.at[:, cols], out_ref.at[i], sems.at[i])
            for i, ref in enumerate((q_ref, do_ref))
        ]
    )


def other_heads(queries, out_grad):
    return call(
        other_kernel, [IN_HBM, IN_HBM],
        [pltpu.VMEM((2, BLK, HALF), BF16)], [queries, out_grad],
        [pltpu.SemaphoreType.DMA((2,))], moved=1 << 20,
    )[0]


def side_parity(core, side):
    return core if side == 0 else 1 - core


def first_place(core, side, small):
    return 4 if small else side_parity(core, side)


def gather_keys(core, sources, which, group, buf):
    for j, kv in enumerate(sources):
        for side in range(2):
            place = 2 * j + side_parity(core, side)
            buf[group, place] = kv[side, which, :, group * HD : (group + 1) * HD]


def write_bias(lengths, chip, core, side, small, bias_ref):
    win = 2 if small else WIN
    k_pos = (2 * chip - 4 + first_place(core, side, small)) * BLK + lax.broadcasted_iota(
        jnp.int32, (win * BLK, BLK), 0
    )
    lane = lax.broadcasted_iota(jnp.int32, (1, BLK), 1)
    q_pos = (2 * chip + side_parity(core, side)) * BLK + lane
    begin = jnp.zeros_like(q_pos)
    end = jnp.int32(0)
    for sample in range(8):
        end = end + lengths[0, sample]
        begin = jnp.where(end <= q_pos, end, begin)
    allowed = (k_pos >= begin) & (k_pos <= q_pos)
    bias_ref[side, : win * BLK] = jnp.where(allowed, 0.0, MASKED)


def masked(raw, bias):
    return raw * EXP2_SCALE + jnp.concatenate([bias, bias], axis=1)


def head_pair(own, oth, which, step):
    group, side, pair = place_of(step)
    start = group * WIDTH + pair * COLS
    two = (own if side == 0 else oth)[which, :, start : start + COLS]
    return jnp.concatenate([two[:, :HD], two[:, HD:]], axis=0)


STEPS = 4 * PAIRS


def place_of(step):
    group, rest = divmod(step, 2 * PAIRS)
    return group, 1 - rest // PAIRS, rest % PAIRS


def start_loads(core, q_hbm, do_hbm, oth_hbm, kv_hbm, own, oth, kv, sems):
    cols = lanes(core * HALF, HALF)
    moves = [(ref, kv.at[i]) for i, ref in enumerate(kv_hbm)]
    moves += [(oth_hbm.at[i], oth.at[i]) for i in range(2)]
    moves += [(ref.at[:, cols], own.at[i]) for i, ref in enumerate((q_hbm, do_hbm))]
    copies = [pltpu.make_async_copy(a, b, sems.at[i]) for i, (a, b) in enumerate(moves)]
    for copy in copies:
        copy.start()
    return copies


def window_rows(core, side, small):
    return lanes(first_place(core, side, small) * BLK, (2 if small else WIN) * BLK)


def window(buf, group, core, side, small):
    win = 2 if small else WIN
    return buf[group, pl.ds(first_place(core, side, small), win)].reshape(win * BLK, HD)


def store_parts(core, acc, parts, scale):
    for group in range(2):
        for j, part in enumerate(parts):
            for side in range(2):
                rows = lanes((2 * j + side_parity(core, side)) * BLK, BLK)
                cut = acc[group, rows, :]
                cut = cut if scale is None else cut * scale
                part[side, :, group * HD : (group + 1) * HD] = cut.astype(part.dtype)


def probs_body(small, core, own, others, loads, k_buf, stat_ref, bias_ref, dv_acc):
    win = 2 if small else WIN

    def raw_scores(step):
        if step == PAIRS:
            for load in loads:
                load.wait()
        group, side, _ = place_of(step)
        return dot(window(k_buf, group, core, side, small), head_pair(own, others, 0, step), NT)

    following = raw_scores(0)
    for step in range(STEPS):
        group, side, _ = place_of(step)
        raw = following
        if step + 1 < STEPS:
            following = raw_scores(step + 1)
        scores = masked(raw, bias_ref[side, : win * BLK])
        peak = jnp.max(scores, axis=0, keepdims=True)
        exponent = jnp.exp2(scores - peak)
        over = 1.0 / jnp.sum(exponent, axis=0, keepdims=True)
        stat_ref[0, step : step + 1] = peak
        stat_ref[1, step : step + 1] = over
        probs = (exponent * over).astype(BF16)
        dv_acc[group, window_rows(core, side, small), :] += dot(
            probs, head_pair(own, others, 1, step), NN
        )


def probs_kernel(
    lengths, q_hbm, do_hbm, oth_hbm, kv_two, kv_one, kv_here,
    dv_two, dv_one, dv_here, stat_ref, bias_ref,
    k_buf, dv_acc, own, others, kv, sems,
):
    chip, core = lax.axis_index("x"), lax.axis_index("core")
    loads = start_loads(
        core, q_hbm, do_hbm, oth_hbm, (kv_two, kv_one, kv_here), own, others, kv, sems
    )
    dv_acc[...] = jnp.zeros_like(dv_acc)
    for load in loads[:5]:
        load.wait()
    loads = loads[5:]
    for group in range(2):
        gather_keys(core, [kv.at[i] for i in range(3)], 0, group, k_buf)
    for small in (True, False):
        @pl.when((chip == 0) == small)
        def _():
            for side in range(2):
                write_bias(lengths, chip, core, side, small, bias_ref)
            probs_body(small, core, own, others, loads, k_buf, stat_ref, bias_ref, dv_acc)
    store_parts(core, dv_acc, (dv_two, dv_one, dv_here), None)


def scores_body(
    small, core, own, others, loads, k_buf, v_buf, k_t, stat_ref, bias_ref, dk_acc, dq_buf
):
    win = 2 if small else WIN

    def products(step):
        if step == PAIRS:
            for load in loads:
                load.wait()
        group, side, _ = place_of(step)
        raw = dot(window(k_buf, group, core, side, small), head_pair(own, others, 0, step), NT)
        grad = dot(window(v_buf, group, core, side, small), head_pair(own, others, 1, step), NT)
        return raw, grad

    following = products(0)
    for step in range(STEPS):
        group, side, pair = place_of(step)
        raw, dprobs = following
        if step + 1 < STEPS:
            following = products(step + 1)
        rows = window_rows(core, side, small)
        peak, over = stat_ref[0, step : step + 1], stat_ref[1, step : step + 1]
        scores = masked(raw, bias_ref[side, : win * BLK])
        probs = jnp.exp2(scores - peak) * over
        delta = jnp.sum(probs * dprobs, axis=0, keepdims=True)
        dscores = (probs * (dprobs - delta)).astype(BF16)
        dk_acc[group, rows, :] += dot(dscores, head_pair(own, others, 0, step), NN)
        dq_t = dot(k_t[group, :, rows], dscores, NN) * SCALE
        for i in range(2):
            start = group * WIDTH + (2 * pair + i) * HD
            dq = dq_t[:, i * BLK : (i + 1) * BLK].T.astype(BF16)
            dq_buf[side, :, start : start + HD] = dq


def scores_kernel(
    lengths, q_hbm, do_hbm, oth_hbm, kv_two, kv_one, kv_here, stat_ref, bias_ref,
    dq_hbm, sent_hbm, dk_two, dk_one, dk_here,
    k_buf, v_buf, k_t, dk_acc, own, others, kv, sems, dq_buf, out_sems,
):
    chip, core = lax.axis_index("x"), lax.axis_index("core")
    loads = start_loads(
        core, q_hbm, do_hbm, oth_hbm, (kv_two, kv_one, kv_here), own, others, kv, sems
    )
    targets = (dq_hbm.at[:, lanes(core * HALF, HALF)], sent_hbm)
    stores = [
        pltpu.make_async_copy(dq_buf.at[side], target, out_sems.at[side])
        for side, target in enumerate(targets)
    ]
    dk_acc[...] = jnp.zeros_like(dk_acc)
    for load in loads[:5]:
        load.wait()
    loads = loads[5:]
    parts = [kv.at[i] for i in range(3)]
    for group in range(2):
        gather_keys(core, parts, 0, group, k_buf)
        gather_keys(core, parts, 1, group, v_buf)
        k_t[group] = k_buf[group].reshape(SPAN * BLK, HD).T
    for small in (True, False):
        @pl.when((chip == 0) == small)
        def _():
            scores_body(
                small, core, own, others, loads, k_buf, v_buf, k_t, stat_ref, bias_ref, dk_acc,
                dq_buf,
            )
    for store in stores:
        store.start()
    store_parts(core, dk_acc, (dk_two, dk_one, dk_here), SCALE)
    for store in stores:
        store.wait()


PARTS = [pltpu.VMEM((2, BLK, COLS), kind) for kind in (BF16, BF16, F32)]
KEYS = pltpu.VMEM((2, SPAN, BLK, HD), BF16)
TURNED = pltpu.VMEM((2, HD, SPAN * BLK), BF16)
TOTAL = pltpu.VMEM((2, SPAN * BLK, HD), F32)
ROWS = pltpu.VMEM((2, BLK, HALF), BF16)
OWN = [ROWS, ROWS, pltpu.VMEM((3, 2, 2, BLK, COLS), BF16), pltpu.SemaphoreType.DMA((7,))]
PRODUCT = 2 * 16 * 2 * BLK * WIN * BLK * HD
OPERANDS = [IN_SMEM] + [IN_HBM] * 6


def attention_probs(operands):
    stats = pltpu.VMEM((2, STEPS, 2 * BLK), F32)
    bias = pltpu.VMEM((2, WIN * BLK, BLK), F32)
    return call(
        probs_kernel, OPERANDS[:4] + [IN_VMEM] + OPERANDS[5:],
        PARTS + [stats, bias], operands,
        [KEYS, TOTAL] + OWN, flops=2 * PRODUCT, exps=PRODUCT // 256, moved=4 << 20, room=16,
    )


def attention_scores(operands, stats, bias):
    return call(
        scores_kernel, OPERANDS + [IN_VMEM] * 2,
        [pltpu.HBM((BLK, width), BF16) for width in (2 * HALF, HALF)] + PARTS,
        [*operands, stats, bias],
        [KEYS, KEYS, TURNED, TOTAL] + OWN
        + [pltpu.VMEM((2, BLK, HALF), BF16), pltpu.SemaphoreType.DMA((2,))],
        flops=4 * PRODUCT, exps=PRODUCT // 256, moved=4 << 20, room=16,
    )


def weight_rows(z, x, dv, side, y):
    sources = [lax.rem(z + 4 - back, 4) for back in range(4)]
    x_rows = jnp.concatenate([x[source, y] for source in sources], axis=0)
    return dot(x_rows, jnp.concatenate([ref[side] for ref in dv], axis=0), TN)


def weight_own_kernel(x, *refs):
    z = lax.axis_index("z")
    for y in range(4):
        refs[-1][y * FEAT : (y + 1) * FEAT] = weight_rows(z, x, refs[:-1], 0, y)


def weight_all_kernel(x, past, *refs):
    z = lax.axis_index("z")
    for y in range(4):
        rows = slice(y * FEAT, (y + 1) * FEAT)
        refs[-1][rows] = (past[rows] + weight_rows(z, x, refs[:-1], 1, y)).astype(BF16)


def weight_part(x_own, x_oth, dv):
    flops = 4 * FEAT * COLS * 8 * BLK
    past = call(
        weight_own_kernel, [IN_VMEM] * 5, [pltpu.VMEM((4 * FEAT, COLS), F32)],
        [x_own, *dv], flops=flops, moved=4 << 20, room=12,
    )[0]
    return call(
        weight_all_kernel, [IN_VMEM] * 6, [pltpu.VMEM((4 * FEAT, COLS), BF16)],
        [x_oth, past, *dv], flops=flops, moved=4 << 20, room=12,
    )[0]


def weight_sum_kernel(got, out_ref):
    for side in range(2):
        total = got[side].astype(F32)
        for source in range(1, 16):
            total = total + got[2 * source + side].astype(F32)
        out_ref[:, side * COLS : (side + 1) * COLS] = total * (1.0 / math.sqrt(16 * LEN))


def weight_sum(got):
    return pl.pallas_call(
        weight_sum_kernel,
        in_specs=[IN_VMEM],
        out_specs=IN_VMEM,
        out_shape=jax.ShapeDtypeStruct((64, HK * HD), F32),
        compiler_params=pltpu.CompilerParams(vmem_limit_bytes=4 << 20),
        name="weight_sum",
    )(near(got))


def sum_kernel(here, one, two, out_ref):
    out_ref[...] = (here[...] + one[...].astype(F32) + two[...].astype(F32)).astype(BF16)


def part_sum(parts):
    return call(sum_kernel, [IN_VMEM] * 3, [pltpu.VMEM((2, BLK, COLS), BF16)], parts)[0]


def finish_kernel(dq_kept, dq_got, dk, dv, got, query_grad, key_grad, value_grad, sems):
    core = lax.axis_index("core")
    other = lanes((1 - core) * HALF, HALF)
    keep_kv, other_kv = lanes(core * COLS, COLS), lanes((1 - core) * COLS, COLS)
    moves = [
        (dq_got, query_grad.at[:, other]),
        (dk.at[0], key_grad.at[:, keep_kv]),
        (got.at[0], key_grad.at[:, other_kv]),
        (dv.at[0], value_grad.at[:, keep_kv]),
        (got.at[1], value_grad.at[:, other_kv]),
    ]
    run_copies(
        [pltpu.make_async_copy(a, b, sems.at[i]) for i, (a, b) in enumerate(moves)]
    )


def finish(dq_kept, dq_got, dk, dv, got):
    outs = [jax.ShapeDtypeStruct((BLK, width * HD), BF16) for width in (HQ, HK, HK)]
    return call(
        finish_kernel, [IN_HBM] + [ANYWHERE] * 4, outs,
        [dq_kept, dq_got, dk, dv, got], [pltpu.SemaphoreType.DMA((5,))], moved=2 << 20,
        aliases={0: 0},
    )


def exchange(value, axes):
    return lax.all_to_all(value, axes, 0, 0, tiled=True)


def shards(queries, key_states, value_states, out_grad, layer_input, lengths):
    core = lax.axis_index("core")
    queries, out_grad = queries[0], out_grad[0]

    def pairs(a, b, which, width):
        cut = [lax.dynamic_slice(v, (0, which * width), (BLK, width)) for v in (a, b)]
        return jnp.stack(cut)

    kv_keep = pairs(key_states[0], value_states[0], core, COLS)
    kv_send = pairs(key_states[0], value_states[0], 1 - core, COLS)
    kv_here = jnp.stack([kv_keep, lax.ppermute(kv_send, "core", SWAP)])
    kv_one = lax.ppermute(kv_here, "x", [(0, 1), (1, 2), (2, 3)])
    kv_two = lax.ppermute(kv_one, "x", [(1, 2), (2, 3)])

    others = lax.ppermute(other_heads(queries, out_grad), "core", SWAP)

    x_own = exchange(pack(layer_input[0]), "z")
    x_oth = lax.ppermute(x_own, "core", SWAP)

    operands = (lengths, queries, out_grad, others, kv_two, kv_one, kv_here)
    dv_two, dv_one, dv_here, stats, bias = attention_probs(operands)
    dq_kept, dq_sent, dk_two, dk_one, dk_here = attention_scores(operands, stats, bias)

    def summed(here, one, two):
        one = lax.ppermute(one, "x", [(1, 0), (2, 1), (3, 2)])
        two = lax.ppermute(two, "x", [(2, 0), (3, 1)])
        return part_sum([here, one, two])

    dv = summed(dv_here, dv_one, dv_two)
    dv_z = [dv] + [
        lax.ppermute(dv, "z", [(i, (i + away) % 4) for i in range(4)]) for away in (1, 2, 3)
    ]
    weight = weight_part(x_own, x_oth, dv_z)
    weight = weight_sum(exchange(weight.reshape(32, 64, COLS), ("y", "x", "core")))

    dk = summed(dk_here, dk_one, dk_two)
    dq_got = lax.ppermute(dq_sent, "core", SWAP)
    got = lax.ppermute(jnp.stack([dk[1], dv[1]]), "core", SWAP)
    query_grad, key_grad, value_grad = finish(dq_kept, dq_got, dk, dv, got)
    return query_grad[None], key_grad[None], value_grad[None], weight


def solution(mesh):
    whole = Mesh(mesh.devices.reshape(4, 4, 4, 2), ("y", "z", "x", "core"))
    rows = P(("y", "z"), ("x", "core"), None)
    return jax.shard_map(
        shards,
        mesh=whole,
        in_specs=(rows,) * 5 + (P(("y", "z"), None),),
        out_specs=(rows,) * 3 + (P(("y", "z", "x", "core"), None),),
        check_vma=False,
    )
```

```python
import math

import jax
import jax.numpy as jnp
from jax import lax
from jax.experimental import pallas as pl
from jax.experimental.pallas import tpu as pltpu
from jax.sharding import Mesh, PartitionSpec as P


D = 8192
HQ = 32
HK = 4
HD = 128
LEN = 1024
BLK = 128
SPAN = 6
WIN = 5
GROUP = HQ // HK
PAIRS = GROUP // 2
WIDTH = GROUP * HD
HALF = HQ * HD // 2
COLS = 2 * HD
FEAT = D // 16
SCALE = HD ** (-0.5)
EXP2_SCALE = SCALE * math.log2(math.e)
MASKED = -1e30
NT = (((1,), (1,)), ((), ()))
NN = (((1,), (0,)), ((), ()))
TN = (((0,), (0,)), ((), ()))
SWAP = [(0, 1), (1, 0)]
BF16 = jnp.bfloat16
F32 = jnp.float32
IN_HBM = pl.BlockSpec(memory_space=pltpu.HBM)
IN_SMEM = pl.BlockSpec(memory_space=pltpu.SMEM)
IN_VMEM = pl.BlockSpec(memory_space=pltpu.VMEM)
ANYWHERE = pl.BlockSpec(memory_space=pltpu.VMEM)


def dot(a, b, dims):
    return lax.dot_general(a, b, dims, preferred_element_type=F32)


def near(value):
    return pltpu.with_memory_space_constraint(value, pltpu.VMEM)


def far(value):
    return pltpu.with_memory_space_constraint(value, pltpu.HBM)


def lanes(start, size):
    return pl.ds(pl.multiple_of(start, HD), size)


def call(kernel, in_specs, outs, operands, scratch=(), flops=0, exps=0, moved=1 << 20, room=4, aliases=None):
    out_specs = [
        IN_HBM if getattr(o, "memory_space", None) != pltpu.VMEM else IN_VMEM for o in outs
    ]
    place = {id(IN_VMEM): near, id(IN_HBM): far}
    operands = [place.get(id(spec), lambda a: a)(a) for a, spec in zip(operands, in_specs)]
    return pl.pallas_call(
        kernel,
        in_specs=list(in_specs),
        out_specs=out_specs,
        out_shape=list(outs),
        scratch_shapes=list(scratch),
        cost_estimate=pl.CostEstimate(flops=flops, transcendentals=exps, bytes_accessed=moved),
        compiler_params=pltpu.CompilerParams(vmem_limit_bytes=room << 20),
        input_output_aliases=aliases or {},
    )(*operands)


def run_copies(copies):
    for copy in copies:
        copy.start()
    for copy in copies:
        copy.wait()


def pack_kernel(x_ref, out_ref, buf, load_sems, store_sems):
    loads, stores = [], []
    for z in range(4):
        for y in range(4):
            cols = pl.ds((y * 4 + z) * FEAT, FEAT)
            at = buf.at[z, y]
            loads.append(pltpu.make_async_copy(x_ref.at[:, cols], at, load_sems.at[4 * z + y]))
            stores.append(pltpu.make_async_copy(at, out_ref.at[z, y], store_sems.at[4 * z + y]))
    for load in loads:
        load.start()
    for load, store in zip(loads, stores):
        load.wait()
        store.start()
    for store in stores:
        store.wait()


def pack(layer_input):
    shape = (4, 4, BLK, FEAT)
    return call(
        pack_kernel, [IN_HBM], [pltpu.HBM(shape, BF16)], [layer_input],
        [pltpu.VMEM(shape, BF16)] + [pltpu.SemaphoreType.DMA((16,))] * 2, moved=4 << 20,
    )[0]


def other_kernel(q_ref, do_ref, out_ref, sems):
    cols = lanes((1 - lax.axis_index("core")) * HALF, HALF)
    run_copies(
        [
            pltpu.make_async_copy(ref.at[:, cols], out_ref.at[i], sems.at[i])
            for i, ref in enumerate((q_ref, do_ref))
        ]
    )


def other_heads(queries, out_grad):
    return call(
        other_kernel, [IN_HBM, IN_HBM],
        [pltpu.VMEM((2, BLK, HALF), BF16)], [queries, out_grad],
        [pltpu.SemaphoreType.DMA((2,))], moved=1 << 20,
    )[0]


def side_parity(core, side):
    return core + side - 2 * core * side


def first_place(core, side, small):
    return 4 if small else side_parity(core, side)


def gather_keys(core, sources, which, group, buf):
    for j, kv in enumerate(sources):
        for side in range(2):
            place = 2 * j + side_parity(core, side)
            buf[group, place] = kv[side, which, :, group * HD : (group + 1) * HD]


def write_bias(lengths, chip, core, side, small, bias_ref):
    win = 2 if small else WIN
    k_pos = (2 * chip - 4 + first_place(core, side, small)) * BLK + lax.broadcasted_iota(
        jnp.int32, (win * BLK, BLK), 0
    )
    lane = lax.broadcasted_iota(jnp.int32, (1, BLK), 1)
    q_pos = (2 * chip + side_parity(core, side)) * BLK + lane
    begin = jnp.zeros_like(q_pos)
    end = jnp.int32(0)
    for sample in range(8):
        end = end + lengths[0, sample]
        begin = jnp.where(end <= q_pos, end, begin)
    allowed = (k_pos >= begin) & (k_pos <= q_pos)
    bias_ref[side, : win * BLK] = jnp.where(allowed, 0.0, MASKED)


def masked(raw, bias):
    return raw * EXP2_SCALE + jnp.concatenate([bias, bias], axis=1)


def head_pair(rows, which, side, group, pair):
    two = rows[side, which, :, lanes(group * WIDTH + pair * COLS, COLS)]
    return jnp.concatenate([two[:, :HD], two[:, HD:]], axis=0)


def for_each_block(body):
    def one(at, carry):
        body(at, 1 - at // 2, at % 2)
        return carry

    lax.fori_loop(0, 4, one, 0)


def start_loads(core, q_hbm, do_hbm, oth_hbm, kv_hbm, rows, kv, sems):
    cols = lanes(core * HALF, HALF)
    moves = [(ref, kv.at[i]) for i, ref in enumerate(kv_hbm)]
    moves += [(oth_hbm.at[i], rows.at[1, i]) for i in range(2)]
    moves += [(ref.at[:, cols], rows.at[0, i]) for i, ref in enumerate((q_hbm, do_hbm))]
    copies = [pltpu.make_async_copy(a, b, sems.at[i]) for i, (a, b) in enumerate(moves)]
    for copy in copies:
        copy.start()
    return copies


def window_rows(core, side, small):
    return lanes(first_place(core, side, small) * BLK, (2 if small else WIN) * BLK)


def window(buf, group, core, side, small):
    win = 2 if small else WIN
    return buf[group, pl.ds(first_place(core, side, small), win)].reshape(win * BLK, HD)


def store_parts(core, acc, parts, scale):
    for group in range(2):
        for j, part in enumerate(parts):
            for side in range(2):
                rows = lanes((2 * j + side_parity(core, side)) * BLK, BLK)
                cut = acc[group, rows, :]
                cut = cut if scale is None else cut * scale
                part[side, :, group * HD : (group + 1) * HD] = cut.astype(part.dtype)


def probs_body(small, core, rows, k_buf, stat_ref, bias_ref, dv_acc):
    win = 2 if small else WIN

    def block(at, side, group):
        def raw_scores(pair):
            keys = window(k_buf, group, core, side, small)
            return dot(keys, head_pair(rows, 0, side, group, pair), NT)

        following = raw_scores(0)
        for pair in range(PAIRS):
            raw = following
            if pair + 1 < PAIRS:
                following = raw_scores(pair + 1)
            scores = masked(raw, bias_ref[side, : win * BLK])
            peak = jnp.max(scores, axis=0, keepdims=True)
            exponent = jnp.exp2(scores - peak)
            over = 1.0 / jnp.sum(exponent, axis=0, keepdims=True)
            stat_ref[at, 0, pair : pair + 1] = peak
            stat_ref[at, 1, pair : pair + 1] = over
            probs = (exponent * over).astype(BF16)
            dv_acc[group, window_rows(core, side, small), :] += dot(
                probs, head_pair(rows, 1, side, group, pair), NN
            )

    for_each_block(block)


def probs_kernel(
    lengths, q_hbm, do_hbm, oth_hbm, kv_two, kv_one, kv_here,
    dv_two, dv_one, dv_here, stat_ref, bias_ref,
    k_buf, dv_acc, rows, kv, sems,
):
    chip, core = lax.axis_index("x"), lax.axis_index("core")
    loads = start_loads(
        core, q_hbm, do_hbm, oth_hbm, (kv_two, kv_one, kv_here), rows, kv, sems
    )
    dv_acc[...] = jnp.zeros_like(dv_acc)
    for load in loads:
        load.wait()
    for group in range(2):
        gather_keys(core, [kv.at[i] for i in range(3)], 0, group, k_buf)
    for small in (True, False):
        @pl.when((chip == 0) == small)
        def _():
            for side in range(2):
                write_bias(lengths, chip, core, side, small, bias_ref)
            probs_body(small, core, rows, k_buf, stat_ref, bias_ref, dv_acc)
    store_parts(core, dv_acc, (dv_two, dv_one, dv_here), None)


def scores_body(small, core, rows, k_buf, v_buf, k_t, stat_ref, bias_ref, dk_acc, dq_buf):
    win = 2 if small else WIN

    def block(at, side, group):
        def products(pair):
            keys = window(k_buf, group, core, side, small)
            values = window(v_buf, group, core, side, small)
            raw = dot(keys, head_pair(rows, 0, side, group, pair), NT)
            return raw, dot(values, head_pair(rows, 1, side, group, pair), NT)

        following = products(0)
        span = window_rows(core, side, small)
        for pair in range(PAIRS):
            raw, dprobs = following
            if pair + 1 < PAIRS:
                following = products(pair + 1)
            peak, over = stat_ref[at, 0, pair : pair + 1], stat_ref[at, 1, pair : pair + 1]
            scores = masked(raw, bias_ref[side, : win * BLK])
            probs = jnp.exp2(scores - peak) * over
            delta = jnp.sum(probs * dprobs, axis=0, keepdims=True)
            dscores = (probs * (dprobs - delta)).astype(BF16)
            dk_acc[group, span, :] += dot(dscores, head_pair(rows, 0, side, group, pair), NN)
            dq_t = dot(k_t[group, :, span], dscores, NN) * SCALE
            dq = [dq_t[:, i * BLK : (i + 1) * BLK].T.astype(BF16) for i in range(2)]
            dq_buf[side, :, lanes(group * WIDTH + pair * COLS, COLS)] = jnp.concatenate(dq, axis=1)

    for_each_block(block)


def scores_kernel(
    lengths, q_hbm, do_hbm, oth_hbm, kv_two, kv_one, kv_here, stat_ref, bias_ref,
    dq_hbm, sent_hbm, dk_two, dk_one, dk_here,
    k_buf, v_buf, k_t, dk_acc, rows, kv, sems, dq_buf, out_sems,
):
    chip, core = lax.axis_index("x"), lax.axis_index("core")
    loads = start_loads(
        core, q_hbm, do_hbm, oth_hbm, (kv_two, kv_one, kv_here), rows, kv, sems
    )
    targets = (dq_hbm.at[:, lanes(core * HALF, HALF)], sent_hbm)
    stores = [
        pltpu.make_async_copy(dq_buf.at[side], target, out_sems.at[side])
        for side, target in enumerate(targets)
    ]
    dk_acc[...] = jnp.zeros_like(dk_acc)
    for load in loads:
        load.wait()
    parts = [kv.at[i] for i in range(3)]
    for group in range(2):
        gather_keys(core, parts, 0, group, k_buf)
        gather_keys(core, parts, 1, group, v_buf)
        k_t[group] = k_buf[group].reshape(SPAN * BLK, HD).T
    for small in (True, False):
        @pl.when((chip == 0) == small)
        def _():
            scores_body(
                small, core, rows, k_buf, v_buf, k_t, stat_ref, bias_ref, dk_acc, dq_buf
            )
    for store in stores:
        store.start()
    store_parts(core, dk_acc, (dk_two, dk_one, dk_here), SCALE)
    for store in stores:
        store.wait()


PARTS = [pltpu.VMEM((2, BLK, COLS), kind) for kind in (BF16, BF16, F32)]
KEYS = pltpu.VMEM((2, SPAN, BLK, HD), BF16)
TURNED = pltpu.VMEM((2, HD, SPAN * BLK), BF16)
TOTAL = pltpu.VMEM((2, SPAN * BLK, HD), F32)
OWN = [pltpu.VMEM((2, 2, BLK, HALF), BF16), pltpu.VMEM((3, 2, 2, BLK, COLS), BF16), pltpu.SemaphoreType.DMA((7,))]
PRODUCT = 2 * 16 * 2 * BLK * WIN * BLK * HD
OPERANDS = [IN_SMEM] + [IN_HBM] * 6


def attention_probs(operands):
    stats = pltpu.VMEM((4, 2, PAIRS, 2 * BLK), F32)
    bias = pltpu.VMEM((2, WIN * BLK, BLK), F32)
    return call(
        probs_kernel, OPERANDS[:4] + [IN_VMEM] + OPERANDS[5:],
        PARTS + [stats, bias], operands,
        [KEYS, TOTAL] + OWN, flops=2 * PRODUCT, exps=PRODUCT // 256, moved=4 << 20, room=16,
    )


def attention_scores(operands, stats, bias):
    return call(
        scores_kernel, OPERANDS + [IN_VMEM] * 2,
        [pltpu.HBM((BLK, width), BF16) for width in (2 * HALF, HALF)] + PARTS,
        [*operands, stats, bias],
        [KEYS, KEYS, TURNED, TOTAL] + OWN
        + [pltpu.VMEM((2, BLK, HALF), BF16), pltpu.SemaphoreType.DMA((2,))],
        flops=4 * PRODUCT, exps=PRODUCT // 256, moved=4 << 20, room=16,
    )


def weight_rows(z, x, dv, side, y):
    sources = [lax.rem(z + 4 - back, 4) for back in range(4)]
    x_rows = jnp.concatenate([x[source, y] for source in sources], axis=0)
    return dot(x_rows, jnp.concatenate([ref[side] for ref in dv], axis=0), TN)


def weight_own_kernel(x, *refs):
    z = lax.axis_index("z")
    for y in range(4):
        refs[-1][y * FEAT : (y + 1) * FEAT] = weight_rows(z, x, refs[:-1], 0, y)


def weight_all_kernel(x, past, *refs):
    z = lax.axis_index("z")
    for y in range(4):
        rows = slice(y * FEAT, (y + 1) * FEAT)
        refs[-1][rows] = (past[rows] + weight_rows(z, x, refs[:-1], 1, y)).astype(BF16)


def weight_part(x_own, x_oth, dv):
    flops = 4 * FEAT * COLS * 8 * BLK
    past = call(
        weight_own_kernel, [IN_VMEM] * 5, [pltpu.VMEM((4 * FEAT, COLS), F32)],
        [x_own, *dv], flops=flops, moved=4 << 20, room=12,
    )[0]
    return call(
        weight_all_kernel, [IN_VMEM] * 6, [pltpu.VMEM((4 * FEAT, COLS), BF16)],
        [x_oth, past, *dv], flops=flops, moved=4 << 20, room=12,
    )[0]


def weight_sum_kernel(got, out_ref):
    for side in range(2):
        total = got[side].astype(F32)
        for source in range(1, 16):
            total = total + got[2 * source + side].astype(F32)
        out_ref[:, side * COLS : (side + 1) * COLS] = total * (1.0 / math.sqrt(16 * LEN))


def weight_sum(got):
    return pl.pallas_call(
        weight_sum_kernel,
        in_specs=[IN_VMEM],
        out_specs=IN_VMEM,
        out_shape=jax.ShapeDtypeStruct((64, HK * HD), F32),
        compiler_params=pltpu.CompilerParams(vmem_limit_bytes=4 << 20),
        name="weight_sum",
    )(near(got))


def sum_kernel(here, one, two, out_ref):
    out_ref[...] = (here[...] + one[...].astype(F32) + two[...].astype(F32)).astype(BF16)


def part_sum(parts):
    return call(sum_kernel, [IN_VMEM] * 3, [pltpu.VMEM((2, BLK, COLS), BF16)], parts)[0]


def finish_kernel(dq_kept, dq_got, dk, dv, got, query_grad, key_grad, value_grad, sems):
    core = lax.axis_index("core")
    other = lanes((1 - core) * HALF, HALF)
    keep_kv, other_kv = lanes(core * COLS, COLS), lanes((1 - core) * COLS, COLS)
    moves = [
        (dq_got, query_grad.at[:, other]),
        (dk.at[0], key_grad.at[:, keep_kv]),
        (got.at[0], key_grad.at[:, other_kv]),
        (dv.at[0], value_grad.at[:, keep_kv]),
        (got.at[1], value_grad.at[:, other_kv]),
    ]
    run_copies(
        [pltpu.make_async_copy(a, b, sems.at[i]) for i, (a, b) in enumerate(moves)]
    )


def finish(dq_kept, dq_got, dk, dv, got):
    outs = [jax.ShapeDtypeStruct((BLK, width * HD), BF16) for width in (HQ, HK, HK)]
    return call(
        finish_kernel, [IN_HBM] + [ANYWHERE] * 4, outs,
        [dq_kept, dq_got, dk, dv, got], [pltpu.SemaphoreType.DMA((5,))], moved=2 << 20,
        aliases={0: 0},
    )


def exchange(value, axes):
    return lax.all_to_all(value, axes, 0, 0, tiled=True)


def shards(queries, key_states, value_states, out_grad, layer_input, lengths):
    core = lax.axis_index("core")
    queries, out_grad = queries[0], out_grad[0]

    def pairs(a, b, which, width):
        cut = [lax.dynamic_slice(v, (0, which * width), (BLK, width)) for v in (a, b)]
        return jnp.stack(cut)

    kv_keep = pairs(key_states[0], value_states[0], core, COLS)
    kv_send = pairs(key_states[0], value_states[0], 1 - core, COLS)
    kv_here = jnp.stack([kv_keep, lax.ppermute(kv_send, "core", SWAP)])
    kv_one = lax.ppermute(kv_here, "x", [(0, 1), (1, 2), (2, 3)])
    kv_two = lax.ppermute(kv_one, "x", [(1, 2), (2, 3)])

    others = lax.ppermute(other_heads(queries, out_grad), "core", SWAP)

    x_own = exchange(pack(layer_input[0]), "z")
    x_oth = lax.ppermute(x_own, "core", SWAP)

    operands = (lengths, queries, out_grad, others, kv_two, kv_one, kv_here)
    dv_two, dv_one, dv_here, stats, bias = attention_probs(operands)
    dq_kept, dq_sent, dk_two, dk_one, dk_here = attention_scores(operands, stats, bias)

    def summed(here, one, two):
        one = lax.ppermute(one, "x", [(1, 0), (2, 1), (3, 2)])
        two = lax.ppermute(two, "x", [(2, 0), (3, 1)])
        return part_sum([here, one, two])

    dv = summed(dv_here, dv_one, dv_two)
    dv_z = [dv] + [
        lax.ppermute(dv, "z", [(i, (i + away) % 4) for i in range(4)]) for away in (1, 2, 3)
    ]
    weight = weight_part(x_own, x_oth, dv_z)
    weight = weight_sum(exchange(weight.reshape(32, 64, COLS), ("y", "x", "core")))

    dk = summed(dk_here, dk_one, dk_two)
    dq_got = lax.ppermute(dq_sent, "core", SWAP)
    got = lax.ppermute(jnp.stack([dk[1], dv[1]]), "core", SWAP)
    query_grad, key_grad, value_grad = finish(dq_kept, dq_got, dk, dv, got)
    return query_grad[None], key_grad[None], value_grad[None], weight


def solution(mesh):
    whole = Mesh(mesh.devices.reshape(4, 4, 4, 2), ("y", "z", "x", "core"))
    rows = P(("y", "z"), ("x", "core"), None)
    return jax.shard_map(
        shards,
        mesh=whole,
        in_specs=(rows,) * 5 + (P(("y", "z"), None),),
        out_specs=(rows,) * 3 + (P(("y", "z", "x", "core"), None),),
        check_vma=False,
    )
```

```python
import math

import jax
import jax.numpy as jnp
from jax import lax
from jax.experimental import pallas as pl
from jax.experimental.pallas import tpu as pltpu
from jax.sharding import Mesh, PartitionSpec as P


D = 8192
HQ = 32
HK = 4
HD = 128
LEN = 1024
BLK = 128
SPAN = 6
WIN = 5
GROUP = HQ // HK
PAIRS = GROUP // 2
WIDTH = GROUP * HD
HALF = HQ * HD // 2
COLS = 2 * HD
FEAT = D // 16
SCALE = HD ** (-0.5)
EXP2_SCALE = SCALE * math.log2(math.e)
MASKED = -1e30
NT = (((1,), (1,)), ((), ()))
NN = (((1,), (0,)), ((), ()))
TN = (((0,), (0,)), ((), ()))
SWAP = [(0, 1), (1, 0)]
BF16 = jnp.bfloat16
F32 = jnp.float32
IN_HBM = pl.BlockSpec(memory_space=pltpu.HBM)
IN_SMEM = pl.BlockSpec(memory_space=pltpu.SMEM)
IN_VMEM = pl.BlockSpec(memory_space=pltpu.VMEM)
ANYWHERE = pl.BlockSpec(memory_space=pltpu.VMEM)


def dot(a, b, dims):
    return lax.dot_general(a, b, dims, preferred_element_type=F32)


def near(value):
    return pltpu.with_memory_space_constraint(value, pltpu.VMEM)


def far(value):
    return pltpu.with_memory_space_constraint(value, pltpu.HBM)


def lanes(start, size):
    return pl.ds(pl.multiple_of(start, HD), size)


def call(kernel, in_specs, outs, operands, scratch=(), flops=0, exps=0, moved=1 << 20, room=4, aliases=None):
    out_specs = [
        IN_HBM if getattr(o, "memory_space", None) != pltpu.VMEM else IN_VMEM for o in outs
    ]
    place = {id(IN_VMEM): near, id(IN_HBM): far}
    operands = [place.get(id(spec), lambda a: a)(a) for a, spec in zip(operands, in_specs)]
    return pl.pallas_call(
        kernel,
        in_specs=list(in_specs),
        out_specs=out_specs,
        out_shape=list(outs),
        scratch_shapes=list(scratch),
        cost_estimate=pl.CostEstimate(flops=flops, transcendentals=exps, bytes_accessed=moved),
        compiler_params=pltpu.CompilerParams(vmem_limit_bytes=room << 20),
        input_output_aliases=aliases or {},
    )(*operands)


def run_copies(copies):
    for copy in copies:
        copy.start()
    for copy in copies:
        copy.wait()


def pack_kernel(x_ref, out_ref, buf, load_sems, store_sems):
    loads, stores = [], []
    for z in range(4):
        for y in range(4):
            cols = pl.ds((y * 4 + z) * FEAT, FEAT)
            at = buf.at[z, y]
            loads.append(pltpu.make_async_copy(x_ref.at[:, cols], at, load_sems.at[4 * z + y]))
            stores.append(pltpu.make_async_copy(at, out_ref.at[z, y], store_sems.at[4 * z + y]))
    for load in loads:
        load.start()
    for load, store in zip(loads, stores):
        load.wait()
        store.start()
    for store in stores:
        store.wait()


def pack(layer_input):
    shape = (4, 4, BLK, FEAT)
    return call(
        pack_kernel, [IN_HBM], [pltpu.HBM(shape, BF16)], [layer_input],
        [pltpu.VMEM(shape, BF16)] + [pltpu.SemaphoreType.DMA((16,))] * 2, moved=4 << 20,
    )[0]


def other_kernel(q_ref, do_ref, out_ref, sems):
    cols = lanes((1 - lax.axis_index("core")) * HALF, HALF)
    run_copies(
        [
            pltpu.make_async_copy(ref.at[:, cols], out_ref.at[i], sems.at[i])
            for i, ref in enumerate((q_ref, do_ref))
        ]
    )


def other_heads(queries, out_grad):
    return call(
        other_kernel, [IN_HBM, IN_HBM],
        [pltpu.VMEM((2, BLK, HALF), BF16)], [queries, out_grad],
        [pltpu.SemaphoreType.DMA((2,))], moved=1 << 20,
    )[0]


def side_parity(core, side):
    return core if side == 0 else 1 - core


def first_place(core, side, small):
    return 4 if small else side_parity(core, side)


def gather_keys(core, sources, which, group, buf):
    for j, kv in enumerate(sources):
        for side in range(2):
            place = 2 * j + side_parity(core, side)
            buf[group, place] = kv[side, which, :, group * HD : (group + 1) * HD]


def write_bias(lengths, chip, core, side, small, bias_ref):
    win = 2 if small else WIN
    k_pos = (2 * chip - 4 + first_place(core, side, small)) * BLK + lax.broadcasted_iota(
        jnp.int32, (win * BLK, BLK), 0
    )
    lane = lax.broadcasted_iota(jnp.int32, (1, BLK), 1)
    q_pos = (2 * chip + side_parity(core, side)) * BLK + lane
    begin = jnp.zeros_like(q_pos)
    end = jnp.int32(0)
    for sample in range(8):
        end = end + lengths[0, sample]
        begin = jnp.where(end <= q_pos, end, begin)
    allowed = (k_pos >= begin) & (k_pos <= q_pos)
    bias_ref[side, : win * BLK] = jnp.where(allowed, 0.0, MASKED)


def masked(raw, bias):
    return raw * EXP2_SCALE + jnp.concatenate([bias, bias], axis=1)


def head_pair(own, oth, which, step):
    group, side, pair = place_of(step)
    start = group * WIDTH + pair * COLS
    two = (own if side == 0 else oth)[which, :, start : start + COLS]
    return jnp.concatenate([two[:, :HD], two[:, HD:]], axis=0)


STEPS = 4 * PAIRS


def place_of(step):
    group, rest = divmod(step, 2 * PAIRS)
    return group, 1 - rest // PAIRS, rest % PAIRS


def start_loads(core, q_hbm, do_hbm, oth_hbm, kv_hbm, own, oth, kv, sems):
    cols = lanes(core * HALF, HALF)
    moves = [(ref, kv.at[i]) for i, ref in enumerate(kv_hbm)]
    moves += [(oth_hbm.at[i], oth.at[i]) for i in range(2)]
    moves += [(ref.at[:, cols], own.at[i]) for i, ref in enumerate((q_hbm, do_hbm))]
    copies = [pltpu.make_async_copy(a, b, sems.at[i]) for i, (a, b) in enumerate(moves)]
    for copy in copies:
        copy.start()
    return copies


def window_rows(core, side, small):
    return lanes(first_place(core, side, small) * BLK, (2 if small else WIN) * BLK)


def window(buf, group, core, side, small):
    win = 2 if small else WIN
    return buf[group, pl.ds(first_place(core, side, small), win)].reshape(win * BLK, HD)


def store_parts(core, acc, parts, scale):
    for group in range(2):
        for j, part in enumerate(parts):
            for side in range(2):
                rows = lanes((2 * j + side_parity(core, side)) * BLK, BLK)
                cut = acc[group, rows, :]
                cut = cut if scale is None else cut * scale
                part[side, :, group * HD : (group + 1) * HD] = cut.astype(part.dtype)


def probs_body(small, core, own, others, loads, k_buf, stat_ref, bias_ref, dv_acc):
    win = 2 if small else WIN

    def raw_scores(step):
        if step == 1:
            loads[0].wait()
        if step == PAIRS:
            for load in loads[1:]:
                load.wait()
        group, side, _ = place_of(step)
        return dot(window(k_buf, group, core, side, small), head_pair(own, others, 0, step), NT)

    following = raw_scores(0)
    for step in range(STEPS):
        group, side, _ = place_of(step)
        raw = following
        if step + 1 < STEPS:
            following = raw_scores(step + 1)
        scores = masked(raw, bias_ref[side, : win * BLK])
        peak = jnp.max(scores, axis=0, keepdims=True)
        exponent = jnp.exp2(scores - peak)
        over = 1.0 / jnp.sum(exponent, axis=0, keepdims=True)
        stat_ref[0, step : step + 1] = peak
        stat_ref[1, step : step + 1] = over
        probs = (exponent * over).astype(BF16)
        dv_acc[group, window_rows(core, side, small), :] += dot(
            probs, head_pair(own, others, 1, step), NN
        )


def probs_kernel(
    lengths, q_hbm, do_hbm, oth_hbm, kv_two, kv_one, kv_here,
    dv_two, dv_one, dv_here, stat_ref, bias_ref, own, others, kv,
    k_buf, dv_acc, sems,
):
    chip, core = lax.axis_index("x"), lax.axis_index("core")
    loads = start_loads(
        core, q_hbm, do_hbm, oth_hbm, (kv_two, kv_one, kv_here), own, others, kv, sems
    )
    dv_acc[...] = jnp.zeros_like(dv_acc)
    for load in loads[:4]:
        load.wait()
    loads = loads[4:]
    for group in range(2):
        gather_keys(core, [kv.at[i] for i in range(3)], 0, group, k_buf)
    for small in (True, False):
        @pl.when((chip == 0) == small)
        def _():
            for side in range(2):
                write_bias(lengths, chip, core, side, small, bias_ref)
            probs_body(small, core, own, others, loads, k_buf, stat_ref, bias_ref, dv_acc)
    store_parts(core, dv_acc, (dv_two, dv_one, dv_here), None)


def scores_body(
    small, core, own, others, k_buf, v_buf, k_t, stat_ref, bias_ref, dk_acc, dq_buf
):
    win = 2 if small else WIN

    def products(step):
        group, side, _ = place_of(step)
        raw = dot(window(k_buf, group, core, side, small), head_pair(own, others, 0, step), NT)
        grad = dot(window(v_buf, group, core, side, small), head_pair(own, others, 1, step), NT)
        return raw, grad

    following = products(0)
    for step in range(STEPS):
        group, side, pair = place_of(step)
        raw, dprobs = following
        if step + 1 < STEPS:
            following = products(step + 1)
        rows = window_rows(core, side, small)
        peak, over = stat_ref[0, step : step + 1], stat_ref[1, step : step + 1]
        scores = masked(raw, bias_ref[side, : win * BLK])
        probs = jnp.exp2(scores - peak) * over
        delta = jnp.sum(probs * dprobs, axis=0, keepdims=True)
        dscores = (probs * (dprobs - delta)).astype(BF16)
        dk_acc[group, rows, :] += dot(dscores, head_pair(own, others, 0, step), NN)
        dq_t = dot(k_t[group, :, rows], dscores, NN) * SCALE
        for i in range(2):
            start = group * WIDTH + (2 * pair + i) * HD
            dq = dq_t[:, i * BLK : (i + 1) * BLK].T.astype(BF16)
            dq_buf[side, :, start : start + HD] = dq


def scores_kernel(
    stat_ref, bias_ref, own, others, kv,
    dq_hbm, sent_hbm, dk_two, dk_one, dk_here,
    k_buf, v_buf, k_t, dk_acc, dq_buf, out_sems,
):
    chip, core = lax.axis_index("x"), lax.axis_index("core")
    targets = (dq_hbm.at[:, lanes(core * HALF, HALF)], sent_hbm)
    stores = [
        pltpu.make_async_copy(dq_buf.at[side], target, out_sems.at[side])
        for side, target in enumerate(targets)
    ]
    dk_acc[...] = jnp.zeros_like(dk_acc)
    parts = [kv.at[i] for i in range(3)]
    for group in range(2):
        gather_keys(core, parts, 0, group, k_buf)
        gather_keys(core, parts, 1, group, v_buf)
        k_t[group] = k_buf[group].reshape(SPAN * BLK, HD).T
    for small in (True, False):
        @pl.when((chip == 0) == small)
        def _():
            scores_body(
                small, core, own, others, k_buf, v_buf, k_t, stat_ref, bias_ref, dk_acc,
                dq_buf,
            )
    for store in stores:
        store.start()
    store_parts(core, dk_acc, (dk_two, dk_one, dk_here), SCALE)
    for store in stores:
        store.wait()


PARTS = [pltpu.VMEM((2, BLK, COLS), kind) for kind in (BF16, BF16, F32)]
KEYS = pltpu.VMEM((2, SPAN, BLK, HD), BF16)
TURNED = pltpu.VMEM((2, HD, SPAN * BLK), BF16)
TOTAL = pltpu.VMEM((2, SPAN * BLK, HD), F32)
ROWS = pltpu.VMEM((2, BLK, HALF), BF16)
LOADED = [ROWS, ROWS, pltpu.VMEM((3, 2, 2, BLK, COLS), BF16)]
PRODUCT = 2 * 16 * 2 * BLK * WIN * BLK * HD
OPERANDS = [IN_SMEM] + [IN_HBM] * 6


def attention_probs(operands):
    stats = pltpu.VMEM((2, STEPS, 2 * BLK), F32)
    bias = pltpu.VMEM((2, WIN * BLK, BLK), F32)
    return call(
        probs_kernel, OPERANDS[:4] + [IN_VMEM] + OPERANDS[5:],
        PARTS + [stats, bias] + LOADED, operands,
        [KEYS, TOTAL, pltpu.SemaphoreType.DMA((7,))], flops=2 * PRODUCT, exps=PRODUCT // 256, moved=4 << 20, room=16,
    )


def attention_scores(kept):
    return call(
        scores_kernel, [IN_VMEM] * 5,
        [pltpu.HBM((BLK, width), BF16) for width in (2 * HALF, HALF)] + PARTS,
        kept,
        [KEYS, KEYS, TURNED, TOTAL]
        + [pltpu.VMEM((2, BLK, HALF), BF16), pltpu.SemaphoreType.DMA((2,))],
        flops=4 * PRODUCT, exps=PRODUCT // 256, moved=4 << 20, room=16,
    )


def weight_rows(z, x, dv, side, y):
    sources = [lax.rem(z + 4 - back, 4) for back in range(4)]
    x_rows = jnp.concatenate([x[source, y] for source in sources], axis=0)
    return dot(x_rows, jnp.concatenate([ref[side] for ref in dv], axis=0), TN)


def weight_own_kernel(x, *refs):
    z = lax.axis_index("z")
    for y in range(4):
        refs[-1][y * FEAT : (y + 1) * FEAT] = weight_rows(z, x, refs[:-1], 0, y)


def weight_all_kernel(x, past, *refs):
    z = lax.axis_index("z")
    for y in range(4):
        rows = slice(y * FEAT, (y + 1) * FEAT)
        refs[-1][rows] = (past[rows] + weight_rows(z, x, refs[:-1], 1, y)).astype(BF16)


def weight_part(x_own, x_oth, dv):
    flops = 4 * FEAT * COLS * 8 * BLK
    past = call(
        weight_own_kernel, [IN_VMEM] * 5, [pltpu.VMEM((4 * FEAT, COLS), F32)],
        [x_own, *dv], flops=flops, moved=4 << 20, room=12,
    )[0]
    return call(
        weight_all_kernel, [IN_VMEM] * 6, [pltpu.VMEM((4 * FEAT, COLS), BF16)],
        [x_oth, past, *dv], flops=flops, moved=4 << 20, room=12,
    )[0]


def weight_sum_kernel(got, out_ref):
    for side in range(2):
        total = got[side].astype(F32)
        for source in range(1, 16):
            total = total + got[2 * source + side].astype(F32)
        out_ref[:, side * COLS : (side + 1) * COLS] = total * (1.0 / math.sqrt(16 * LEN))


def weight_sum(got):
    return pl.pallas_call(
        weight_sum_kernel,
        in_specs=[IN_VMEM],
        out_specs=IN_VMEM,
        out_shape=jax.ShapeDtypeStruct((64, HK * HD), F32),
        compiler_params=pltpu.CompilerParams(vmem_limit_bytes=4 << 20),
        name="weight_sum",
    )(near(got))


def sum_kernel(here, one, two, out_ref):
    out_ref[...] = (here[...] + one[...].astype(F32) + two[...].astype(F32)).astype(BF16)


def part_sum(parts):
    return call(sum_kernel, [IN_VMEM] * 3, [pltpu.VMEM((2, BLK, COLS), BF16)], parts)[0]


def finish_kernel(dq_kept, dq_got, dk, dv, got, query_grad, key_grad, value_grad, sems):
    core = lax.axis_index("core")
    other = lanes((1 - core) * HALF, HALF)
    keep_kv, other_kv = lanes(core * COLS, COLS), lanes((1 - core) * COLS, COLS)
    moves = [
        (dq_got, query_grad.at[:, other]),
        (dk.at[0], key_grad.at[:, keep_kv]),
        (got.at[0], key_grad.at[:, other_kv]),
        (dv.at[0], value_grad.at[:, keep_kv]),
        (got.at[1], value_grad.at[:, other_kv]),
    ]
    run_copies(
        [pltpu.make_async_copy(a, b, sems.at[i]) for i, (a, b) in enumerate(moves)]
    )


def finish(dq_kept, dq_got, dk, dv, got):
    outs = [jax.ShapeDtypeStruct((BLK, width * HD), BF16) for width in (HQ, HK, HK)]
    return call(
        finish_kernel, [IN_HBM] + [ANYWHERE] * 4, outs,
        [dq_kept, dq_got, dk, dv, got], [pltpu.SemaphoreType.DMA((5,))], moved=2 << 20,
        aliases={0: 0},
    )


def exchange(value, axes):
    return lax.all_to_all(value, axes, 0, 0, tiled=True)


def shards(queries, key_states, value_states, out_grad, layer_input, lengths):
    core = lax.axis_index("core")
    queries, out_grad = queries[0], out_grad[0]

    def pairs(a, b, which, width):
        cut = [lax.dynamic_slice(v, (0, which * width), (BLK, width)) for v in (a, b)]
        return jnp.stack(cut)

    kv_keep = pairs(key_states[0], value_states[0], core, COLS)
    kv_send = pairs(key_states[0], value_states[0], 1 - core, COLS)
    kv_here = jnp.stack([kv_keep, lax.ppermute(kv_send, "core", SWAP)])
    kv_one = lax.ppermute(kv_here, "x", [(0, 1), (1, 2), (2, 3)])
    kv_two = lax.ppermute(kv_one, "x", [(1, 2), (2, 3)])

    others = lax.ppermute(other_heads(queries, out_grad), "core", SWAP)

    x_own = exchange(pack(layer_input[0]), "z")
    x_oth = lax.ppermute(x_own, "core", SWAP)

    operands = (lengths, queries, out_grad, others, kv_two, kv_one, kv_here)
    dv_two, dv_one, dv_here, *kept = attention_probs(operands)
    dq_kept, dq_sent, dk_two, dk_one, dk_here = attention_scores(kept)

    def summed(here, one, two):
        one = lax.ppermute(one, "x", [(1, 0), (2, 1), (3, 2)])
        two = lax.ppermute(two, "x", [(2, 0), (3, 1)])
        return part_sum([here, one, two])

    dv = summed(dv_here, dv_one, dv_two)
    dv_z = [dv] + [
        lax.ppermute(dv, "z", [(i, (i + away) % 4) for i in range(4)]) for away in (1, 2, 3)
    ]
    weight = weight_part(x_own, x_oth, dv_z)
    weight = weight_sum(exchange(weight.reshape(32, 64, COLS), ("y", "x", "core")))

    dk = summed(dk_here, dk_one, dk_two)
    dq_got = lax.ppermute(dq_sent, "core", SWAP)
    got = lax.ppermute(jnp.stack([dk[1], dv[1]]), "core", SWAP)
    query_grad, key_grad, value_grad = finish(dq_kept, dq_got, dk, dv, got)
    return query_grad[None], key_grad[None], value_grad[None], weight


def solution(mesh):
    whole = Mesh(mesh.devices.reshape(4, 4, 4, 2), ("y", "z", "x", "core"))
    rows = P(("y", "z"), ("x", "core"), None)
    return jax.shard_map(
        shards,
        mesh=whole,
        in_specs=(rows,) * 5 + (P(("y", "z"), None),),
        out_specs=(rows,) * 3 + (P(("y", "z", "x", "core"), None),),
        check_vma=False,
    )
```
